32 devices in a mesh: ens: 2 (over x), lat: 4 (over z), lon: 4 (over y, core).
Axes of the slice: x: 2, y: 2, z: 4, core: 2. Of those that a mesh axis runs over, the one named last changes fastest.
Arguments:
- prior_states: bfloat16 [16, 40, 128, 1024], P('ens', None, 'lat', 'lon'), may hold values from -6 to 6
- measured_brightness: float32 [16, 64, 512], P(None, 'lat', 'lon'), may hold values from -16 to 16
- measured_indicator: int32 [64, 512], P('lat', 'lon'), may hold values 0 or 1
- sensor_error_spread: float32 [16], replicated, may hold values from 2 to 8
- entry_layer_stencil: bfloat16 [64, 40, 5, 5], replicated, may hold values from -0.25 to 0.25
- entry_layer_offset: float32 [64], replicated, may hold values from -3 to 3
- middle_layer_stencil: bfloat16 [64, 64, 3, 3], replicated, may hold values from -0.375 to 0.375
- middle_layer_offset: float32 [64], replicated, may hold values from -3 to 3
- brightness_matrix: bfloat16 [16, 64], replicated, may hold values from -0.75 to 0.75
- brightness_offset: float32 [16], replicated, may hold values from -3 to 3
- ancestor_indices: int32 [16, 4, 8], P(None, 'lat', 'lon'), may hold values from 0 to 15, as said below
Outputs:
- analysis: float32 [16, 40, 128, 1024], P('ens', None, 'lat', 'lon')
- weights: float32 [16, 64, 512], P('ens', 'lat', 'lon')
The draws below stay inside these ranges and needn't reach their ends.
Inputs may be any that keep to these rules, and one draw needn't show every extreme that they name: `ancestor_indices`: in every localization tile, the 8 slots s with the same s // 8 take at most 4 parents from any one group of particles with the same p // 8, and exactly 4 from some group.
All inputs are finite; a program needn't handle non-finite values. No bound on the sum of `measured_indicator` on one device may be relied on, other than what follows from the above.
Results may differ from the reference program's by a relative error of at most 0.0085.
Values may be sent and summed in bfloat16 or wider, within the bound.
No kernel may reach another device: no remote copies, remote signals or barrier semaphores. Data moves between devices by JAX's collectives and lax.ppermute only.
A program may use at most 128 MiB of HBM per device.

```python
import math
import jax
import jax.numpy as jnp
from jax import lax

STATE_HEIGHTS = 40
CH = 64
OCH = 16
P_DEV = 8
PATCH_NORTHWARD = 32
PATCH_EASTWARD = 128
RADIUS = 16
ENSEMBLE_SIZE = 16
MESH_NORTHWARD = 128
MESH_EASTWARD = 1024
NOLAT = 64
NOLON = 512
CAP = 4


def draw_ancestor_indices(key, part):
    groups = ENSEMBLE_SIZE // P_DEV
    tile_count = MESH_NORTHWARD // PATCH_NORTHWARD * (MESH_EASTWARD // PATCH_EASTWARD)
    group_keys = jax.random.split(jax.random.fold_in(key, 11), groups * tile_count)

    def one_group(group_key):
        key_favored, key_score, key_shuffle, key_local = jax.random.split(group_key, 4)
        favored = jax.random.randint(key_favored, (), 0, groups)
        seat_source = jnp.arange(groups * CAP, dtype=jnp.int32) // CAP
        seat_score = jax.random.randint(key_score, (groups * CAP,), 0, 1 << 16) + jnp.where(seat_source == favored, 0, 1 << 17)
        seat_score = seat_score * (groups * CAP) + jnp.arange(groups * CAP, dtype=jnp.int32)
        seat_order = jnp.argsort(seat_score, stable=True)
        chosen = seat_source[seat_order[:P_DEV]]
        chosen = jax.random.permutation(key_shuffle, chosen)
        local_index = jax.random.randint(key_local, (P_DEV,), 0, P_DEV)
        return (chosen * P_DEV + local_index).astype(jnp.int32)
    parent_ids = jax.vmap(one_group)(group_keys)
    parent_ids = parent_ids.reshape(groups, MESH_NORTHWARD // PATCH_NORTHWARD, MESH_EASTWARD // PATCH_EASTWARD, P_DEV)
    return jnp.transpose(parent_ids, (0, 3, 1, 2)).reshape(ENSEMBLE_SIZE, MESH_NORTHWARD // PATCH_NORTHWARD, MESH_EASTWARD // PATCH_EASTWARD)


def draw_measured_brightness(key, part):
    noise_field = jax.random.normal(jax.random.fold_in(key, 5), (OCH, NOLAT, NOLON), jnp.float32)
    row_index = jnp.arange(NOLAT, dtype=jnp.int32)
    in_band = (row_index // RADIUS % 4 == 1).astype(jnp.float32)
    band_level = jax.random.uniform(jax.random.fold_in(key, 9), (OCH, 1, 1), jnp.float32, 8.0, 10.0)
    noise_field = noise_field + band_level * in_band[None, :, None]
    return jnp.clip(noise_field, -16.0, 16.0)


def set_ends(drawn, rng, low, high):
    longest = drawn.shape.index(max(drawn.shape))
    spots = []
    for shift in (0, 1):
        where = [jax.random.randint(jax.random.fold_in(rng, axis), (), 0, length) for axis, length in enumerate(drawn.shape)]
        where[longest] = (where[longest] + shift) % drawn.shape[longest]
        spots.append(tuple(where))
    return drawn.at[spots[0]].set(low).at[spots[1]].set(high)


def level_of(key, shape, cuts, low, largest):
    def one(dim, blocks):
        steps = jax.random.uniform(jax.random.fold_in(jax.random.fold_in(key, 6), dim), (blocks,), jnp.float32, low / len(cuts), largest / len(cuts))
        return jnp.repeat(jnp.exp(steps), shape[dim] // blocks).reshape((-1,) + (1,) * (len(shape) - dim - 1))

    factor_of = one(*cuts[0])
    for cut in cuts[1:]:
        factor_of = factor_of * one(*cut)
    return factor_of


def noise(rng, dims, scale, most, cuts=(), held_as=jnp.bfloat16):
    entries = scale * jax.random.normal(rng, dims, jnp.float32)
    if cuts:
        entries = entries * level_of(rng, dims, cuts, -0.22, 0.18)
    return jnp.clip(entries, -most, most).astype(held_as)


def setup_inputs(seed: int = 0) -> dict:
    streams_of = jax.random.split(jax.random.key(seed), 12)
    return {
        "prior_states": noise(streams_of[0], (ENSEMBLE_SIZE, STATE_HEIGHTS, MESH_NORTHWARD, MESH_EASTWARD), 1.0, 6.0, ((0, 2), (2, 4), (3, 4))),
        "measured_brightness": draw_measured_brightness(jax.random.fold_in(streams_of[11], 71), 0),
        "measured_indicator": set_ends((jax.random.randint(streams_of[2], (NOLAT, NOLON), 0, 4) < 3).astype(jnp.int32), jax.random.fold_in(streams_of[2], 1), 0, 1),
        "sensor_error_spread": jnp.clip(jnp.exp(jax.random.uniform(streams_of[3], (OCH,), jnp.float32, math.log(2.0), math.log(8.0))), 2.0, 8.0),
        "entry_layer_stencil": noise(streams_of[4], (CH, STATE_HEIGHTS, 5, 5), (STATE_HEIGHTS * 12) ** -0.5, 0.25),
        "entry_layer_offset": noise(streams_of[5], (CH,), 0.5, 3.0, (), jnp.float32),
        "middle_layer_stencil": noise(streams_of[6], (CH, CH, 3, 3), (CH * 4) ** -0.5, 0.375),
        "middle_layer_offset": noise(streams_of[7], (CH,), 0.5, 3.0, (), jnp.float32),
        "brightness_matrix": noise(streams_of[8], (OCH, CH), CH ** -0.5, 0.75),
        "brightness_offset": noise(streams_of[9], (OCH,), 0.5, 3.0, (), jnp.float32),
        "ancestor_indices": draw_ancestor_indices(jax.random.fold_in(streams_of[11], 71), 0),
    }


relax_factor = 0.6


def taper_band(inner_count, radius):
    tap_count = 2 * radius + 1
    offsets = jnp.arange(tap_count, dtype=jnp.float32) - radius
    tap_width = radius / 2.0
    tap_total = jnp.sum(jnp.exp(-0.5 * (offsets / tap_width) ** 2))
    out_index = jnp.arange(inner_count, dtype=jnp.int32)[:, None]
    in_index = jnp.arange(inner_count + 2 * radius, dtype=jnp.int32)[None, :]
    offset_index = in_index - out_index
    inside = (offset_index >= 0) & (offset_index < tap_count)
    shifted = (offset_index - radius).astype(jnp.float32)
    values = jnp.exp(-0.5 * (shifted / tap_width) ** 2) / tap_total
    return jnp.where(inside, values, 0.0)


def expand_patches(values):
    lead = values.shape[:-2]
    rows, cols = values.shape[-2], values.shape[-1]
    grown = jnp.broadcast_to(values[..., :, None, :, None], lead + (rows, 2, cols, 2))
    return grown.reshape(lead + (rows * 2, cols * 2))


def network(member, entry_layer_stencil, entry_layer_offset, middle_layer_stencil, middle_layer_offset, brightness_matrix, brightness_offset):
    numbers = ("NCHW", "OIHW", "NCHW")
    highest = lax.Precision.HIGHEST
    first_layer = lax.conv_general_dilated(member[None].astype(jnp.float32), entry_layer_stencil.astype(jnp.float32), (2, 2), ((2, 2), (2, 2)), dimension_numbers=numbers, precision=highest)[0]
    first_layer = jax.nn.relu(first_layer + entry_layer_offset[:, None, None]).astype(jnp.bfloat16)
    second_layer = lax.conv_general_dilated(first_layer[None].astype(jnp.float32), middle_layer_stencil.astype(jnp.float32), (1, 1), ((2, 2), (2, 2)), rhs_dilation=(2, 2), dimension_numbers=numbers, precision=highest)[0]
    second_layer = jax.nn.relu(second_layer + middle_layer_offset[:, None, None]).astype(jnp.bfloat16)
    return jnp.einsum("oc,cij->oij", brightness_matrix.astype(jnp.float32), second_layer.astype(jnp.float32), precision=highest) + brightness_offset[:, None, None]


def reference(prior_states, measured_brightness, measured_indicator, sensor_error_spread, entry_layer_stencil, entry_layer_offset, middle_layer_stencil, middle_layer_offset, brightness_matrix, brightness_offset, ancestor_indices):
    highest = lax.Precision.HIGHEST
    mask_values = measured_indicator.astype(jnp.float32)

    def departure_from_truth(member):
        predicted = network(member, entry_layer_stencil, entry_layer_offset, middle_layer_stencil, middle_layer_offset, brightness_matrix, brightness_offset)
        innovation = measured_brightness - predicted
        return jnp.sum(innovation * innovation / sensor_error_spread[:, None, None], axis=0) * mask_values

    departure_power_two = lax.map(departure_from_truth, prior_states)
    padded = jnp.pad(departure_power_two, ((0, 0), (RADIUS, RADIUS), (RADIUS, RADIUS)))
    band_lat = taper_band(NOLAT, RADIUS)
    band_lon = taper_band(NOLON, RADIUS)
    lat_smooth = jnp.einsum("ij,pjk->pik", band_lat, padded, precision=highest)
    smooth = jnp.einsum("pij,kj->pik", lat_smooth, band_lon, precision=highest)
    log_weight = -0.5 * smooth
    log_peak = jnp.max(log_weight, axis=0)
    normed_departure = jnp.exp(log_weight - log_peak[None])
    denominator = jnp.sum(normed_departure, axis=0)
    weights = normed_departure / denominator[None]

    def gather_totals_step(running, entry_pair):
        member, member_share = entry_pair
        return running + expand_patches(member_share)[None] * member.astype(jnp.float32), None

    likelihood_product, ignored_result = lax.scan(gather_totals_step, jnp.zeros((STATE_HEIGHTS, MESH_NORTHWARD, MESH_EASTWARD), jnp.float32), (prior_states, normed_departure))
    weighted_mean = likelihood_product / expand_patches(denominator)[None]
    patchwise_state = prior_states.reshape(ENSEMBLE_SIZE, STATE_HEIGHTS, MESH_NORTHWARD // PATCH_NORTHWARD, PATCH_NORTHWARD, MESH_EASTWARD // PATCH_EASTWARD, PATCH_EASTWARD)
    lat_tile = jnp.arange(MESH_NORTHWARD // PATCH_NORTHWARD, dtype=jnp.int32)[:, None]
    lon_tile = jnp.arange(MESH_EASTWARD // PATCH_EASTWARD, dtype=jnp.int32)[None, :]

    def member_update(parent_row):
        taken = patchwise_state[parent_row.astype(jnp.int32), :, lat_tile, :, lon_tile, :]
        taken = jnp.transpose(taken, (2, 0, 3, 1, 4)).reshape(STATE_HEIGHTS, MESH_NORTHWARD, MESH_EASTWARD).astype(jnp.float32)
        return weighted_mean + relax_factor * (taken - weighted_mean)

    analysis = lax.map(member_update, ancestor_indices)
    return analysis, weights
```

```python
import functools

import jax
import jax.numpy as jnp
from jax import lax
from jax.experimental import pallas as pl
from jax.experimental.pallas import tpu as pltpu
from jax.sharding import PartitionSpec as P

PATCH_NORTHWARD = 32
PATCH_EASTWARD = 128
RADIUS = 16


relax_factor = 0.6


def extended(shard, sides, width):
    for axis, dim in sides:
        peers, length = (lax.axis_size(axis), shard.shape[dim])
        up = [(i, (i + 1) % peers) for i in range(peers - 1)]
        down = [(j, i) for i, j in up]
        last = lax.slice_in_dim(shard, length - width, length, axis=dim)
        first = lax.slice_in_dim(shard, 0, width, axis=dim)
        before = lax.ppermute(last, axis, up)
        after = lax.ppermute(first, axis, down)
        shard = jnp.concatenate([before, shard, after], axis=dim)
    return shard


def taper_band(inner_count, radius):
    tap_count = 2 * radius + 1
    offsets = jnp.arange(tap_count, dtype=jnp.float32) - radius
    tap_width = radius / 2.0
    tap_total = jnp.sum(jnp.exp(-0.5 * (offsets / tap_width) ** 2))
    out_index = jnp.arange(inner_count, dtype=jnp.int32)[:, None]
    in_index = jnp.arange(inner_count + 2 * radius, dtype=jnp.int32)[None, :]
    offset_index = in_index - out_index
    inside = (offset_index >= 0) & (offset_index < tap_count)
    shifted = (offset_index - radius).astype(jnp.float32)
    values = jnp.exp(-0.5 * (shifted / tap_width) ** 2) / tap_total
    return jnp.where(inside, values, 0.0)


def expand_patches(values):
    lead = values.shape[:-2]
    rows, cols = (values.shape[-2], values.shape[-1])
    grown = jnp.broadcast_to(values[..., :, None, :, None], lead + (rows, 2, cols, 2))
    return grown.reshape(lead + (rows * 2, cols * 2))


def doubled(values):
    rows, cols = values.shape
    to_rows = lax.broadcasted_iota(jnp.int32, (2 * rows, rows), 0) // 2
    of_rows = lax.broadcasted_iota(jnp.int32, (2 * rows, rows), 1)
    tall = (to_rows == of_rows).astype(jnp.float32)
    of_cols = lax.broadcasted_iota(jnp.int32, (cols, 2 * cols), 0)
    to_cols = lax.broadcasted_iota(jnp.int32, (cols, 2 * cols), 1) // 2
    wide = (to_cols == of_cols).astype(jnp.float32)
    grown = jnp.dot(values, wide, precision=lax.Precision.HIGHEST)
    return jnp.dot(tall, grown, precision=lax.Precision.HIGHEST)


def tiles_of(rows, cols):
    return [
        (north, east)
        for north in range(rows // PATCH_NORTHWARD)
        for east in range(cols // PATCH_EASTWARD)
    ]


def tile_window(north, east):
    return (
        pl.ds(north * PATCH_NORTHWARD, PATCH_NORTHWARD),
        pl.ds(east * PATCH_EASTWARD, PATCH_EASTWARD),
    )


def pick_tiles(ancestors, place, prior_states, targets, seats):
    members, heights, rows, cols = prior_states.shape
    tiles = tiles_of(rows, cols)

    def kernel(ancestor, spot, prior, out, sems):
        own = spot[0]

        def transfer(target, seat, member, tile):
            window = tile_window(*tiles[tile])
            return pltpu.make_async_copy(
                prior.at[(member, slice(None)) + window],
                out.at[(target, seat, slice(None)) + window],
                sems.at[target, seat, tile],
            )

        used = {}
        for target in range(targets):
            for tile in range(len(tiles)):
                rank = jnp.int32(0)
                for slot in range(members):
                    parent = ancestor[(spot[1 + target] * members + slot) * len(tiles) + tile]
                    local = parent - own * members
                    hit = (local >= 0) & (local < members) & (rank < seats)

                    @pl.when(hit)
                    def _(target=target, rank=rank, local=local, tile=tile):
                        transfer(target, rank, local, tile).start()

                    rank = rank + hit.astype(jnp.int32)
                used[target, tile] = rank
        for (target, tile), rank in used.items():
            for seat in range(seats):

                @pl.when(seat < rank)
                def _(target=target, seat=seat, tile=tile):
                    transfer(target, seat, 0, tile).wait()

    return pl.pallas_call(
        kernel,
        out_shape=jax.ShapeDtypeStruct((targets, seats, heights, rows, cols), prior_states.dtype),
        in_specs=[
            pl.BlockSpec(memory_space=pltpu.SMEM),
            pl.BlockSpec(memory_space=pltpu.SMEM),
            pl.BlockSpec(memory_space=pltpu.HBM),
        ],
        out_specs=pl.BlockSpec(memory_space=pltpu.HBM),
        scratch_shapes=[pltpu.SemaphoreType.DMA((targets, seats, len(tiles)))],
        name="pick_tiles",
    )(ancestors, place, prior_states)


def group_mean(log_weight, prior_states, chunk):
    members, heights, rows, cols = prior_states.shape
    pixel_rows, pixel_cols = log_weight.shape[1:]

    def kernel(log_ref, prior, scaled_ref, norm_ref, mean_ref, sent_ref, share):
        @pl.when(pl.program_id(0) == 0)
        def _():
            values = log_ref[...]
            peak = jnp.max(values, axis=0)
            scaled = jnp.exp(values - peak[None])
            total = jnp.sum(scaled, axis=0)
            scaled_ref[...] = scaled
            norm_ref[0] = peak
            norm_ref[1] = total
            for member in range(members):
                share[member] = doubled(scaled[member] / total)

        for level in range(chunk):
            mean = share[0] * prior[0, level].astype(jnp.float32)
            for member in range(1, members):
                mean = mean + share[member] * prior[member, level].astype(jnp.float32)
            mean_ref[level] = mean
            sent_ref[level] = mean.astype(jnp.bfloat16)

    return pl.pallas_call(
        kernel,
        grid=(heights // chunk,),
        out_shape=(
            jax.ShapeDtypeStruct(log_weight.shape, jnp.float32),
            jax.ShapeDtypeStruct((2, pixel_rows, pixel_cols), jnp.float32),
            jax.ShapeDtypeStruct((heights, rows, cols), jnp.float32),
            jax.ShapeDtypeStruct((heights, rows, cols), jnp.bfloat16),
        ),
        in_specs=[
            pl.BlockSpec(log_weight.shape, lambda i: (0, 0, 0)),
            pl.BlockSpec((members, chunk, rows, cols), lambda i: (0, i, 0, 0)),
        ],
        out_specs=(
            pl.BlockSpec(log_weight.shape, lambda i: (0, 0, 0)),
            pl.BlockSpec((2, pixel_rows, pixel_cols), lambda i: (0, 0, 0)),
            pl.BlockSpec((chunk, rows, cols), lambda i: (i, 0, 0)),
            pl.BlockSpec((chunk, rows, cols), lambda i: (i, 0, 0)),
        ),
        scratch_shapes=[pltpu.VMEM((members, rows, cols), jnp.float32)],
        compiler_params=pltpu.CompilerParams(vmem_limit_bytes=32 << 20),
        name="group_mean",
    )(log_weight, prior_states)


def combine(ancestors, place, scaled, own_norm, other_norm, own_mean, other_mean, prior_states, received, chunk, shared):
    members, heights, rows, cols = prior_states.shape
    tiles = tiles_of(rows, cols)
    count = len(tiles)
    groups = ancestors.shape[0] // (members * count)
    sources, seats = received.shape[:2]
    received = received.reshape((sources * seats,) + received.shape[2:])
    steps = heights // chunk

    def kernel(
        ancestor, spot, scaled_ref, own_ref, other_ref, mean_ref, peer_ref, prior, remote,
        out, weights, picks, own_share, other_share, table, seen, sems,
    ):
        step = pl.program_id(0)

        def transfer(array, source, at, slot, tile, half):
            window = tile_window(*tiles[tile])
            levels = pl.ds(at * chunk, chunk)
            return pltpu.make_async_copy(
                array.at[(source, levels) + window],
                picks.at[(half, slot, slice(None)) + window],
                sems.at[half, slot, tile],
            )

        def fetch(at, half):
            for slot in range(members):
                for tile in range(count):
                    source = table[slot * count + tile]

                    @pl.when(source < members)
                    def _():
                        transfer(prior, source, at, slot, tile, half).start()

                    @pl.when(source >= members)
                    def _():
                        transfer(remote, source - members, at, slot, tile, half).start()

        @pl.when(step == 0)
        def _():
            own = spot[0]
            for tile in range(count):
                for group in range(groups):
                    seen[group] = 0
                for slot in range(members):
                    parent = ancestor[(own * members + slot) * count + tile]
                    group = lax.div(parent, jnp.int32(members))
                    rank = seen[group]
                    seen[group] = rank + 1
                    line = (jnp.int32(0) if sources == 1 else group) * seats + rank
                    table[slot * count + tile] = jnp.where(
                        group == own, parent - own * members, members + line
                    )
            fetch(0, 0)
            own_peak, own_total = own_ref[0], own_ref[1]
            other_peak, other_total = other_ref[0], other_ref[1]
            peak = jnp.maximum(own_peak, other_peak)
            own_scale = jnp.exp(own_peak - peak)
            if shared:
                total = other_total
            else:
                other_part = other_total * jnp.exp(other_peak - peak)
                total = own_total * own_scale + other_part
                own_share[...] = (1.0 - relax_factor) * doubled(own_total * own_scale / total)
                other_share[...] = (1.0 - relax_factor) * doubled(other_part / total)
            weights[...] = scaled_ref[...] * (own_scale / total)[None]

        @pl.when(step + 1 < steps)
        def _():
            fetch(step + 1, lax.rem(step + 1, 2))

        half = lax.rem(step, 2)
        for slot in range(members):
            for tile in range(count):
                transfer(prior, 0, 0, slot, tile, half).wait()
        for level in range(chunk):
            if shared:
                base = (1.0 - relax_factor) * mean_ref[level]
            else:
                base = own_share[...] * mean_ref[level] + other_share[...] * peer_ref[
                    level
                ].astype(jnp.float32)
            for slot in range(members):
                out[slot, level] = base + relax_factor * picks[half, slot, level].astype(
                    jnp.float32
                )

    small = lambda i: (0, 0, 0)
    return pl.pallas_call(
        kernel,
        grid=(steps,),
        out_shape=(
            jax.ShapeDtypeStruct(prior_states.shape, jnp.float32),
            jax.ShapeDtypeStruct(scaled.shape, jnp.float32),
        ),
        in_specs=[
            pl.BlockSpec(memory_space=pltpu.SMEM),
            pl.BlockSpec(memory_space=pltpu.SMEM),
            pl.BlockSpec(scaled.shape, small),
            pl.BlockSpec(own_norm.shape, small),
            pl.BlockSpec(other_norm.shape, small),
            pl.BlockSpec((chunk, rows, cols), lambda i: (i, 0, 0)),
            pl.BlockSpec((chunk, rows, cols), lambda i: (i, 0, 0)),
            pl.BlockSpec(memory_space=pltpu.HBM),
            pl.BlockSpec(memory_space=pltpu.HBM),
        ],
        out_specs=(
            pl.BlockSpec((members, chunk, rows, cols), lambda i: (0, i, 0, 0)),
            pl.BlockSpec(scaled.shape, small),
        ),
        scratch_shapes=[
            pltpu.VMEM((2, members, chunk, rows, cols), prior_states.dtype),
            pltpu.VMEM((rows, cols), jnp.float32),
            pltpu.VMEM((rows, cols), jnp.float32),
            pltpu.SMEM((members * count,), jnp.int32),
            pltpu.SMEM((groups,), jnp.int32),
            pltpu.SemaphoreType.DMA((2, members, count)),
        ],
        compiler_params=pltpu.CompilerParams(vmem_limit_bytes=32 << 20),
        name="combine",
    )(
        ancestors, place, scaled, own_norm, other_norm, own_mean, other_mean, prior_states, received
    )


def log_weights(
    prior_states,
    measured_brightness,
    measured_indicator,
    sensor_error_spread,
    entry_layer_stencil,
    entry_layer_offset,
    middle_layer_stencil,
    middle_layer_offset,
    brightness_matrix,
    brightness_offset,
):
    numbers = ("NCHW", "OIHW", "NCHW")
    highest = lax.Precision.HIGHEST
    enlarged_state = extended(prior_states, (("lat", 2), ("lon", 3)), 2)
    first_layer = lax.conv_general_dilated(
        enlarged_state,
        entry_layer_stencil,
        (2, 2),
        "VALID",
        dimension_numbers=numbers,
        preferred_element_type=jnp.float32,
    )
    first_layer = jax.nn.relu(first_layer + entry_layer_offset[None, :, None, None]).astype(
        jnp.bfloat16
    )
    first_wide = extended(first_layer, (("lat", 2), ("lon", 3)), 2)
    second_layer = lax.conv_general_dilated(
        first_wide,
        middle_layer_stencil,
        (1, 1),
        "VALID",
        rhs_dilation=(2, 2),
        dimension_numbers=numbers,
        preferred_element_type=jnp.float32,
    )
    second_layer = jax.nn.relu(second_layer + middle_layer_offset[None, :, None, None]).astype(
        jnp.bfloat16
    )
    predicted = (
        jnp.einsum(
            "oc,pcij->poij", brightness_matrix, second_layer, preferred_element_type=jnp.float32
        )
        + brightness_offset[None, :, None, None]
    )
    innovation = measured_brightness[None] - predicted
    departure_power_two = (
        jnp.sum(innovation * innovation / sensor_error_spread[None, :, None, None], axis=1)
        * measured_indicator.astype(jnp.float32)[None]
    )
    band_lat = taper_band(departure_power_two.shape[1], RADIUS)
    band_lon = taper_band(departure_power_two.shape[2], RADIUS)
    padded = extended(departure_power_two, (("lat", 1),), RADIUS)
    lat_smooth = jnp.einsum("ij,pjk->pik", band_lat, padded, precision=highest)
    lat_smooth = extended(lat_smooth, (("lon", 2),), RADIUS)
    smooth = jnp.einsum("pij,kj->pik", lat_smooth, band_lon, precision=highest)
    return -0.5 * smooth


def chunk_of(heights):
    return next(size for size in (5, 4, 2, 1) if heights % size == 0)


def body(prior_states, *rest):
    ancestor_indices = rest[-1]
    members, heights, rows, cols = prior_states.shape
    groups = lax.axis_size("ens")
    own = lax.axis_index("ens").astype(jnp.int32)
    seats = max(2, (members + groups - 1) // groups)
    ancestors = ancestor_indices.reshape(-1)
    swap = [(0, 1), (1, 0)]
    paired = groups == 2
    if paired:
        targets = (1 - own)[None]
    else:
        targets = jnp.arange(groups, dtype=jnp.int32)
    place = jnp.concatenate([own[None], targets])
    outgoing = pick_tiles(ancestors, place, prior_states, targets.shape[0], seats)
    if paired:
        received = lax.ppermute(outgoing, "ens", swap)
    else:
        received = lax.all_to_all(outgoing, "ens", split_axis=0, concat_axis=0, tiled=True)
    log_weight = log_weights(prior_states, *rest[:-1])
    scaled, own_norm, own_mean, sent_mean = group_mean(
        log_weight, prior_states, chunk_of(heights)
    )
    if paired:
        other_norm = lax.ppermute(own_norm, "ens", swap)
        other_mean = lax.ppermute(sent_mean, "ens", swap)
    else:
        peak = lax.pmax(own_norm[0], "ens")
        part = own_norm[1] * jnp.exp(own_norm[0] - peak)
        total, own_mean = lax.psum((part, expand_patches(part)[None] * own_mean), "ens")
        own_mean = own_mean / expand_patches(total)[None]
        other_norm = jnp.stack([peak, total])
        other_mean = sent_mean
    return combine(
        ancestors,
        place,
        scaled,
        own_norm,
        other_norm,
        own_mean,
        other_mean,
        prior_states,
        received,
        chunk_of(heights),
        not paired,
    )


def solution(mesh):
    return jax.shard_map(
        body,
        mesh=mesh,
        in_specs=(
            P("ens", None, "lat", "lon"),
            P(None, "lat", "lon"),
            P("lat", "lon"),
            P(),
            P(),
            P(),
            P(),
            P(),
            P(),
            P(),
            P(None, "lat", "lon"),
        ),
        out_specs=(P("ens", None, "lat", "lon"), P("ens", "lat", "lon")),
        check_vma=False,
    )
```

```python
import functools

import jax
import jax.numpy as jnp
from jax import lax
from jax.experimental import pallas as pl
from jax.experimental.pallas import tpu as pltpu
from jax.sharding import PartitionSpec as P

PATCH_NORTHWARD = 32
PATCH_EASTWARD = 128
RADIUS = 16


relax_factor = 0.6


def extended(shard, sides, width):
    for axis, dim in sides:
        peers, length = (lax.axis_size(axis), shard.shape[dim])
        up = [(i, (i + 1) % peers) for i in range(peers - 1)]
        down = [(j, i) for i, j in up]
        last = lax.slice_in_dim(shard, length - width, length, axis=dim)
        first = lax.slice_in_dim(shard, 0, width, axis=dim)
        before = lax.ppermute(last, axis, up)
        after = lax.ppermute(first, axis, down)
        shard = jnp.concatenate([before, shard, after], axis=dim)
    return shard


def taper_band(inner_count, radius):
    tap_count = 2 * radius + 1
    offsets = jnp.arange(tap_count, dtype=jnp.float32) - radius
    tap_width = radius / 2.0
    tap_total = jnp.sum(jnp.exp(-0.5 * (offsets / tap_width) ** 2))
    out_index = jnp.arange(inner_count, dtype=jnp.int32)[:, None]
    in_index = jnp.arange(inner_count + 2 * radius, dtype=jnp.int32)[None, :]
    offset_index = in_index - out_index
    inside = (offset_index >= 0) & (offset_index < tap_count)
    shifted = (offset_index - radius).astype(jnp.float32)
    values = jnp.exp(-0.5 * (shifted / tap_width) ** 2) / tap_total
    return jnp.where(inside, values, 0.0)


def expand_patches(values):
    lead = values.shape[:-2]
    rows, cols = (values.shape[-2], values.shape[-1])
    grown = jnp.broadcast_to(values[..., :, None, :, None], lead + (rows, 2, cols, 2))
    return grown.reshape(lead + (rows * 2, cols * 2))


def doubled(values):
    rows, cols = values.shape
    to_rows = lax.broadcasted_iota(jnp.int32, (2 * rows, rows), 0) // 2
    of_rows = lax.broadcasted_iota(jnp.int32, (2 * rows, rows), 1)
    tall = (to_rows == of_rows).astype(jnp.float32)
    of_cols = lax.broadcasted_iota(jnp.int32, (cols, 2 * cols), 0)
    to_cols = lax.broadcasted_iota(jnp.int32, (cols, 2 * cols), 1) // 2
    wide = (to_cols == of_cols).astype(jnp.float32)
    grown = jnp.dot(values, wide, precision=lax.Precision.HIGHEST)
    return jnp.dot(tall, grown, precision=lax.Precision.HIGHEST)


def tiles_of(rows, cols):
    return [
        (north, east)
        for north in range(rows // PATCH_NORTHWARD)
        for east in range(cols // PATCH_EASTWARD)
    ]


def tile_window(north, east):
    return (
        pl.ds(north * PATCH_NORTHWARD, PATCH_NORTHWARD),
        pl.ds(east * PATCH_EASTWARD, PATCH_EASTWARD),
    )


def pick_tiles(ancestors, place, prior_states, targets, seats):
    members, heights, rows, cols = prior_states.shape
    tiles = tiles_of(rows, cols)

    def kernel(ancestor, spot, prior, out, sems):
        own = spot[0]

        def transfer(target, seat, member, tile):
            window = tile_window(*tiles[tile])
            return pltpu.make_async_copy(
                prior.at[(member, slice(None)) + window],
                out.at[(target, seat, slice(None)) + window],
                sems.at[target, seat, tile],
            )

        used = {}
        for target in range(targets):
            for tile in range(len(tiles)):
                rank = jnp.int32(0)
                for slot in range(members):
                    parent = ancestor[(spot[1 + target] * members + slot) * len(tiles) + tile]
                    local = parent - own * members
                    hit = (local >= 0) & (local < members) & (rank < seats)

                    @pl.when(hit)
                    def _(target=target, rank=rank, local=local, tile=tile):
                        transfer(target, rank, local, tile).start()

                    rank = rank + hit.astype(jnp.int32)
                used[target, tile] = rank
        for (target, tile), rank in used.items():
            for seat in range(seats):

                @pl.when(seat < rank)
                def _(target=target, seat=seat, tile=tile):
                    transfer(target, seat, 0, tile).wait()

    return pl.pallas_call(
        kernel,
        out_shape=jax.ShapeDtypeStruct((targets, seats, heights, rows, cols), prior_states.dtype),
        in_specs=[
            pl.BlockSpec(memory_space=pltpu.SMEM),
            pl.BlockSpec(memory_space=pltpu.SMEM),
            pl.BlockSpec(memory_space=pltpu.HBM),
        ],
        out_specs=pl.BlockSpec(memory_space=pltpu.VMEM),
        scratch_shapes=[pltpu.SemaphoreType.DMA((targets, seats, len(tiles)))],
        compiler_params=pltpu.CompilerParams(vmem_limit_bytes=32 << 20),
        name="pick_tiles",
    )(ancestors, place, prior_states)


def group_mean(log_weight, prior_states, chunk):
    members, heights, rows, cols = prior_states.shape
    pixel_rows, pixel_cols = log_weight.shape[1:]

    def kernel(log_ref, prior, scaled_ref, norm_ref, mean_ref, sent_ref, share):
        @pl.when(pl.program_id(0) == 0)
        def _():
            values = log_ref[...]
            peak = jnp.max(values, axis=0)
            scaled = jnp.exp(values - peak[None])
            total = jnp.sum(scaled, axis=0)
            scaled_ref[...] = scaled
            norm_ref[0] = peak
            norm_ref[1] = total
            for member in range(members):
                share[member] = doubled(scaled[member] / total)

        for level in range(chunk):
            mean = share[0] * prior[0, level].astype(jnp.float32)
            for member in range(1, members):
                mean = mean + share[member] * prior[member, level].astype(jnp.float32)
            mean_ref[level] = mean
            sent_ref[level] = mean.astype(jnp.bfloat16)

    return pl.pallas_call(
        kernel,
        grid=(heights // chunk,),
        out_shape=(
            jax.ShapeDtypeStruct(log_weight.shape, jnp.float32),
            jax.ShapeDtypeStruct((2, pixel_rows, pixel_cols), jnp.float32),
            jax.ShapeDtypeStruct((heights, rows, cols), jnp.float32),
            jax.ShapeDtypeStruct((heights, rows, cols), jnp.bfloat16),
        ),
        in_specs=[
            pl.BlockSpec(log_weight.shape, lambda i: (0, 0, 0)),
            pl.BlockSpec((members, chunk, rows, cols), lambda i: (0, i, 0, 0)),
        ],
        out_specs=(
            pl.BlockSpec(log_weight.shape, lambda i: (0, 0, 0)),
            pl.BlockSpec((2, pixel_rows, pixel_cols), lambda i: (0, 0, 0)),
            pl.BlockSpec((chunk, rows, cols), lambda i: (i, 0, 0)),
            pl.BlockSpec((chunk, rows, cols), lambda i: (i, 0, 0)),
        ),
        scratch_shapes=[pltpu.VMEM((members, rows, cols), jnp.float32)],
        compiler_params=pltpu.CompilerParams(vmem_limit_bytes=32 << 20),
        name="group_mean",
    )(log_weight, prior_states)


def combine(ancestors, place, scaled, own_norm, other_norm, own_mean, other_mean, prior_states, received, chunk, shared):
    members, heights, rows, cols = prior_states.shape
    tiles = tiles_of(rows, cols)
    count = len(tiles)
    groups = ancestors.shape[0] // (members * count)
    sources, seats = received.shape[:2]
    received = received.reshape((sources * seats,) + received.shape[2:])
    steps = heights // chunk

    def kernel(
        ancestor, spot, scaled_ref, own_ref, other_ref, mean_ref, peer_ref, prior, remote,
        out, weights, picks, own_share, other_share, table, seen, sems,
    ):
        step = pl.program_id(0)

        def transfer(array, source, at, slot, tile, half):
            window = tile_window(*tiles[tile])
            levels = pl.ds(at * chunk, chunk)
            return pltpu.make_async_copy(
                array.at[(source, levels) + window],
                picks.at[(half, slot, slice(None)) + window],
                sems.at[half, slot, tile],
            )

        def fetch(at, half):
            for slot in range(members):
                for tile in range(count):
                    source = table[slot * count + tile]

                    @pl.when(source < members)
                    def _():
                        transfer(prior, source, at, slot, tile, half).start()

                    @pl.when(source >= members)
                    def _():
                        transfer(remote, source - members, at, slot, tile, half).start()

        @pl.when(step == 0)
        def _():
            own = spot[0]
            for tile in range(count):
                for group in range(groups):
                    seen[group] = 0
                for slot in range(members):
                    parent = ancestor[(own * members + slot) * count + tile]
                    group = lax.div(parent, jnp.int32(members))
                    rank = seen[group]
                    seen[group] = rank + 1
                    line = (jnp.int32(0) if sources == 1 else group) * seats + rank
                    table[slot * count + tile] = jnp.where(
                        group == own, parent - own * members, members + line
                    )
            fetch(0, 0)
            own_peak, own_total = own_ref[0], own_ref[1]
            other_peak, other_total = other_ref[0], other_ref[1]
            peak = jnp.maximum(own_peak, other_peak)
            own_scale = jnp.exp(own_peak - peak)
            if shared:
                total = other_total
            else:
                other_part = other_total * jnp.exp(other_peak - peak)
                total = own_total * own_scale + other_part
                own_share[...] = (1.0 - relax_factor) * doubled(own_total * own_scale / total)
                other_share[...] = (1.0 - relax_factor) * doubled(other_part / total)
            weights[...] = scaled_ref[...] * (own_scale / total)[None]

        @pl.when(step + 1 < steps)
        def _():
            fetch(step + 1, lax.rem(step + 1, 2))

        half = lax.rem(step, 2)
        for slot in range(members):
            for tile in range(count):
                transfer(prior, 0, 0, slot, tile, half).wait()
        for level in range(chunk):
            if shared:
                base = (1.0 - relax_factor) * mean_ref[level]
            else:
                base = own_share[...] * mean_ref[level] + other_share[...] * peer_ref[
                    level
                ].astype(jnp.float32)
            for slot in range(members):
                out[slot, level] = base + relax_factor * picks[half, slot, level].astype(
                    jnp.float32
                )

    small = lambda i: (0, 0, 0)
    return pl.pallas_call(
        kernel,
        grid=(steps,),
        out_shape=(
            jax.ShapeDtypeStruct(prior_states.shape, jnp.float32),
            jax.ShapeDtypeStruct(scaled.shape, jnp.float32),
        ),
        in_specs=[
            pl.BlockSpec(memory_space=pltpu.SMEM),
            pl.BlockSpec(memory_space=pltpu.SMEM),
            pl.BlockSpec(scaled.shape, small),
            pl.BlockSpec(own_norm.shape, small),
            pl.BlockSpec(other_norm.shape, small),
            pl.BlockSpec((chunk, rows, cols), lambda i: (i, 0, 0)),
            pl.BlockSpec((chunk, rows, cols), lambda i: (i, 0, 0)),
            pl.BlockSpec(memory_space=pltpu.HBM),
            pl.BlockSpec(memory_space=pltpu.HBM),
        ],
        out_specs=(
            pl.BlockSpec((members, chunk, rows, cols), lambda i: (0, i, 0, 0)),
            pl.BlockSpec(scaled.shape, small),
        ),
        scratch_shapes=[
            pltpu.VMEM((2, members, chunk, rows, cols), prior_states.dtype),
            pltpu.VMEM((rows, cols), jnp.float32),
            pltpu.VMEM((rows, cols), jnp.float32),
            pltpu.SMEM((members * count,), jnp.int32),
            pltpu.SMEM((groups,), jnp.int32),
            pltpu.SemaphoreType.DMA((2, members, count)),
        ],
        compiler_params=pltpu.CompilerParams(vmem_limit_bytes=32 << 20),
        name="combine",
    )(
        ancestors, place, scaled, own_norm, other_norm, own_mean, other_mean, prior_states, received
    )


SLOTS = 3


def entry_layer(prior_states, even_taps, odd_taps):
    members, heights, rows, cols = prior_states.shape
    channels = odd_taps.shape[0] // 2
    padded = even_taps.shape[1] // 5
    pixel_rows, pixel_cols = rows // 2, cols // 2

    def kernel(prior, even_ref, odd_ref, out, east_ref, west_ref, sorted_cells, lines):
        @pl.when(pl.program_id(0) == 0)
        def _():
            lines[...] = jnp.zeros_like(lines)

        here = lax.broadcasted_iota(jnp.int32, (cols, cols), 0)
        there = lax.broadcasted_iota(jnp.int32, (cols, cols), 1)
        chosen = jnp.where(there < pixel_cols, 2 * there, 2 * (there - pixel_cols) + 1)
        parity = (here == chosen).astype(jnp.float32).astype(jnp.bfloat16)
        split = jnp.dot(
            prior[0].reshape(heights * rows, cols), parity, preferred_element_type=jnp.float32
        )
        for kind in range(2):
            sorted_cells[kind] = split[:, kind * pixel_cols : (kind + 1) * pixel_cols]
        for kind in range(2):
            for row in range(rows):
                lines[kind, row + 4, :heights] = sorted_cells[
                    kind, pl.ds(row, heights, stride=rows), :
                ].astype(jnp.bfloat16)
        east_ref[0] = jnp.zeros_like(east_ref[0])
        west_ref[0] = jnp.zeros_like(west_ref[0])
        lane = lax.broadcasted_iota(jnp.int32, (channels, pixel_cols), 1)
        last = pixel_cols - 1
        for row in range(-1, pixel_rows + 1):
            even, odd = (
                jnp.dot(
                    taps[...],
                    lines[kind, 2 * row + 2 : 2 * row + 7].reshape(5 * padded, pixel_cols),
                    preferred_element_type=jnp.float32,
                )
                for kind, taps in ((0, even_ref), (1, odd_ref))
            )
            ahead = pltpu.roll(even[:channels] + odd[:channels], 1, 1)
            behind = pltpu.roll(even[2 * channels :], last, 1)
            inside = (
                even[channels : 2 * channels]
                + odd[channels:]
                + jnp.where(lane == 0, 0.0, ahead)
                + jnp.where(lane == last, 0.0, behind)
            )
            out[0, row + 1] = inside
            at = 2 * (row + 2)
            east = jnp.where(
                (lane == at) | (lane == at + 1), pltpu.roll(inside, at + 2, 1), east_ref[0]
            )
            east_ref[0] = jnp.where(lane == 64 + at, pltpu.roll(ahead, 64 + at, 1), east)
            west = jnp.where(
                (lane == 64 + at) | (lane == 65 + at), pltpu.roll(inside, 64 + at, 1), west_ref[0]
            )
            west_ref[0] = jnp.where(
                lane == at + 1, pltpu.roll(behind, (at + 2) % pixel_cols, 1), west
            )

    edge = jax.ShapeDtypeStruct((members, channels, pixel_cols), jnp.float32)
    edge_spec = pl.BlockSpec((1, channels, pixel_cols), lambda i: (i, 0, 0))
    return pl.pallas_call(
        kernel,
        grid=(members,),
        out_shape=(
            jax.ShapeDtypeStruct((members, pixel_rows + 2, channels, pixel_cols), jnp.float32),
            edge,
            edge,
        ),
        in_specs=[
            pl.BlockSpec((1, heights, rows, cols), lambda i: (i, 0, 0, 0)),
            pl.BlockSpec(even_taps.shape, lambda i: (0, 0)),
            pl.BlockSpec(odd_taps.shape, lambda i: (0, 0)),
        ],
        out_specs=(
            pl.BlockSpec((1, pixel_rows + 2, channels, pixel_cols), lambda i: (i, 0, 0, 0)),
            edge_spec,
            edge_spec,
        ),
        scratch_shapes=[
            pltpu.VMEM((2, heights * rows, pixel_cols), jnp.float32),
            pltpu.VMEM((2, rows + 8, padded, pixel_cols), jnp.bfloat16),
        ],
        compiler_params=pltpu.CompilerParams(vmem_limit_bytes=40 << 20),
        name="entry_layer",
    )(prior_states, even_taps, odd_taps)


def end_fix(from_west, from_east, lane):
    return jnp.where(lane % 2 == 0, from_west, pltpu.roll(from_east, 62, 1))


def with_ends(values, fix, row, lane):
    moved = pltpu.roll(fix, (60 - 2 * row) % 128, 1)
    return values + jnp.where((lane == 0) | (lane == 127), moved, 0.0)


def side_columns(from_west, from_east, own_east, own_west, lane):
    return jnp.where(lane < 64, from_west + own_west, from_east + own_east)


def row_ends(partial, own_east, own_west, from_west, from_east):
    members, row_count, channels, pixel_cols = partial.shape
    tail = row_count // SLOTS - 1

    def kernel(top, bottom, east, west, left, right, north, south):
        lane = lax.broadcasted_iota(jnp.int32, (channels, pixel_cols), 1)
        for member in range(members):
            inward, outward = left[member], right[member]
            fix = end_fix(inward, outward, lane)
            sides = side_columns(inward, outward, east[member], west[member], lane)
            for slot in range(SLOTS):
                north[member, slot] = with_ends(top[member, slot], fix, slot - 1, lane).astype(
                    jnp.bfloat16
                )
                south[member, slot] = with_ends(
                    bottom[member, slot], fix, row_count - 4 + slot, lane
                ).astype(jnp.bfloat16)
            north[member, SLOTS] = sides.astype(jnp.bfloat16)
            south[member, SLOTS] = sides.astype(jnp.bfloat16)

    edge_spec = pl.BlockSpec((members, channels, pixel_cols), lambda i: (0, 0, 0))
    rows_spec = (members, SLOTS, channels, pixel_cols)
    sent = (members, SLOTS + 1, channels, pixel_cols)
    return pl.pallas_call(
        kernel,
        grid=(1,),
        out_shape=(jax.ShapeDtypeStruct(sent, jnp.bfloat16),) * 2,
        in_specs=[
            pl.BlockSpec(rows_spec, lambda i: (0, 0, 0, 0)),
            pl.BlockSpec(rows_spec, lambda i: (0, tail, 0, 0)),
            edge_spec,
            edge_spec,
            edge_spec,
            edge_spec,
        ],
        out_specs=(pl.BlockSpec(sent, lambda i: (0, 0, 0, 0)),) * 2,
        compiler_params=pltpu.CompilerParams(vmem_limit_bytes=40 << 20),
        name="row_ends",
    )(partial, partial, own_east, own_west, from_west, from_east)


def misfits(
    borders, partial, own_east, own_west, from_west, from_east, from_north, from_south,
    entry_offset, middle_taps, side_taps, middle_offset, matrix, offset, observed, variance, mask,
):
    members, row_count, channels, pixel_cols = partial.shape
    pixel_rows = row_count - 2
    bands = matrix.shape[0]

    def kernel(
        border, pre, east, west, left, right, above, below, bias_ref, taps, side, bias_two,
        matrix_ref, offset_ref, obs, variance_ref, mask_ref, out, hidden, sides,
    ):
        lane = lax.broadcasted_iota(jnp.int32, (channels, pixel_cols), 1)
        bias = bias_ref[...]
        top, bottom = border[0] == 0, border[1] == 0
        start, end = border[2] == 0, border[3] == 0
        keep_top = jnp.where(top, 0.0, 1.0)
        keep_bottom = jnp.where(bottom, 0.0, 1.0)
        fix = end_fix(left[0], right[0], lane)

        def level(values):
            return jnp.maximum(values + bias, 0.0)

        for row in range(-2, pixel_rows + 2):
            if row == -2:
                values = above[0, 0].astype(jnp.float32)
            elif row == pixel_rows + 1:
                values = below[0, SLOTS - 1].astype(jnp.float32)
            else:
                values = with_ends(pre[0, row + 1], fix, row, lane)
                if row <= 0:
                    values = values + above[0, row + 2].astype(jnp.float32)
                if row >= pixel_rows - 1:
                    values = values + below[0, row - pixel_rows + 1].astype(jnp.float32)
            values = level(values)
            if row < 0:
                values = values * keep_top
            if row >= pixel_rows:
                values = values * keep_bottom
            hidden[row + 2] = values.astype(jnp.bfloat16)

        slot = lax.rem(lane, 64) // 2
        cells = side_columns(left[0], right[0], east[0], west[0], lane)
        upper = pltpu.roll(above[0, SLOTS].astype(jnp.float32), 128 - 2 * pixel_rows, 1)
        lower = pltpu.roll(below[0, SLOTS].astype(jnp.float32), 2 * pixel_rows, 1)
        cells = (
            cells
            + jnp.where(slot < 3, upper, 0.0)
            + jnp.where((slot > pixel_rows) & (slot < pixel_rows + 4), lower, 0.0)
        )
        outside = (
            (top & (slot < 2))
            | (bottom & (slot >= pixel_rows + 2))
            | (start & (lane < 64))
            | (end & (lane >= 64))
        )
        cells = jnp.where(outside, 0.0, level(cells))
        stack = jnp.concatenate(
            [pltpu.roll(cells, 4, 1), cells, pltpu.roll(cells, 124, 1)], axis=0
        ).astype(jnp.bfloat16)
        found = jnp.dot(side[...], stack, preferred_element_type=jnp.float32)
        sides[...] = jnp.where(lane < 64, found[:channels], found[channels:])

        for row in range(pixel_rows):
            window = jnp.concatenate([hidden[row], hidden[row + 2], hidden[row + 4]], axis=0)
            parts = jnp.dot(taps[...], window, preferred_element_type=jnp.float32)
            column = sides[...]
            at = 2 * (row + 2)
            values = (
                parts[channels : 2 * channels]
                + jnp.where(
                    lane < 2,
                    pltpu.roll(column, 128 - at, 1),
                    pltpu.roll(parts[:channels], 2, 1),
                )
                + jnp.where(
                    lane >= 126,
                    pltpu.roll(column, 62 - at if at <= 62 else 190 - at, 1),
                    pltpu.roll(parts[2 * channels :], 126, 1),
                )
            )
            second = jnp.maximum(values + bias_two[...], 0.0).astype(jnp.bfloat16)
            predicted = jnp.dot(matrix_ref[...], second, preferred_element_type=jnp.float32)
            misfit = obs[row] - (predicted + offset_ref[...])
            total = jnp.sum(misfit * misfit / variance_ref[...], axis=0, keepdims=True)
            out[0, row : row + 1] = total * mask_ref[row : row + 1].astype(jnp.float32)

    edge_spec = pl.BlockSpec((1, channels, pixel_cols), lambda i: (i, 0, 0))
    line_spec = pl.BlockSpec((1, SLOTS + 1, channels, pixel_cols), lambda i: (i, 0, 0, 0))

    def whole(array):
        return pl.BlockSpec(array.shape, lambda i, n=array.ndim: (0,) * n)

    fixed = (entry_offset, middle_taps, side_taps, middle_offset, matrix, offset, observed)
    fixed = fixed + (variance, mask)
    return pl.pallas_call(
        kernel,
        grid=(members,),
        out_shape=jax.ShapeDtypeStruct((members, pixel_rows, pixel_cols), jnp.float32),
        in_specs=[
            pl.BlockSpec(memory_space=pltpu.SMEM),
            pl.BlockSpec((1, row_count, channels, pixel_cols), lambda i: (i, 0, 0, 0)),
            edge_spec,
            edge_spec,
            edge_spec,
            edge_spec,
            line_spec,
            line_spec,
        ]
        + [whole(array) for array in fixed],
        out_specs=pl.BlockSpec((1, pixel_rows, pixel_cols), lambda i: (i, 0, 0)),
        scratch_shapes=[
            pltpu.VMEM((pixel_rows + 4, channels, pixel_cols), jnp.bfloat16),
            pltpu.VMEM((channels, pixel_cols), jnp.float32),
        ],
        compiler_params=pltpu.CompilerParams(vmem_limit_bytes=40 << 20),
        name="misfits",
    )(
        borders, partial, own_east, own_west, from_west, from_east, from_north, from_south, *fixed
    )


def neighbours(axis):
    count = lax.axis_size(axis)
    onward = [(i, i + 1) for i in range(count - 1)]
    return onward, [(j, i) for i, j in onward]


def departures(
    prior_states,
    measured_brightness,
    measured_indicator,
    sensor_error_spread,
    entry_layer_stencil,
    entry_layer_offset,
    middle_layer_stencil,
    middle_layer_offset,
    brightness_matrix,
    brightness_offset,
):
    channels, heights = entry_layer_stencil.shape[:2]
    padded = (heights + 15) // 16 * 16
    entry = jnp.pad(entry_layer_stencil, ((0, 0), (0, padded - heights), (0, 0), (0, 0)))
    entry = jnp.transpose(entry, (3, 0, 2, 1)).reshape(5, channels, 5 * padded)
    even_taps = jnp.concatenate([entry[0], entry[2], entry[4]])
    odd_taps = jnp.concatenate([entry[1], entry[3]])
    middle = jnp.transpose(middle_layer_stencil, (3, 0, 2, 1)).reshape(3, channels, 3 * channels)
    middle_taps = middle.reshape(3 * channels, 3 * channels)
    side_taps = jnp.concatenate([middle[0], middle[2]])
    lat, lon = lax.axis_index("lat"), lax.axis_index("lon")
    borders = jnp.stack(
        [lat, lax.axis_size("lat") - 1 - lat, lon, lax.axis_size("lon") - 1 - lon]
    ).astype(jnp.int32)
    partial, own_east, own_west = entry_layer(prior_states, even_taps, odd_taps)
    onward, back = neighbours("lon")
    from_west = lax.ppermute(own_east, "lon", onward)
    from_east = lax.ppermute(own_west, "lon", back)
    north, south = row_ends(partial, own_east, own_west, from_west, from_east)
    onward, back = neighbours("lat")
    from_north = lax.ppermute(south, "lat", onward)
    from_south = lax.ppermute(north, "lat", back)
    return misfits(
        borders,
        partial,
        own_east,
        own_west,
        from_west,
        from_east,
        from_north,
        from_south,
        entry_layer_offset[:, None],
        middle_taps,
        side_taps,
        middle_layer_offset[:, None],
        brightness_matrix,
        brightness_offset[:, None],
        jnp.transpose(measured_brightness, (1, 0, 2)),
        sensor_error_spread[:, None],
        measured_indicator,
    )


def log_weights(*arguments):
    highest = lax.Precision.HIGHEST
    departure_power_two = departures(*arguments)
    band_lat = taper_band(departure_power_two.shape[1], RADIUS)
    band_lon = taper_band(departure_power_two.shape[2], RADIUS)
    padded = extended(departure_power_two, (("lat", 1),), RADIUS)
    lat_smooth = jnp.einsum("ij,pjk->pik", band_lat, padded, precision=highest)
    lat_smooth = extended(lat_smooth, (("lon", 2),), RADIUS)
    smooth = jnp.einsum("pij,kj->pik", lat_smooth, band_lon, precision=highest)
    return -0.5 * smooth


def chunk_of(heights):
    return next(size for size in (5, 4, 2, 1) if heights % size == 0)


def body(prior_states, *rest):
    ancestor_indices = rest[-1]
    members, heights, rows, cols = prior_states.shape
    groups = lax.axis_size("ens")
    own = lax.axis_index("ens").astype(jnp.int32)
    seats = max(2, (members + groups - 1) // groups)
    ancestors = ancestor_indices.reshape(-1)
    swap = [(0, 1), (1, 0)]
    paired = groups == 2
    if paired:
        targets = (1 - own)[None]
    else:
        targets = jnp.arange(groups, dtype=jnp.int32)
    place = jnp.concatenate([own[None], targets])
    outgoing = pick_tiles(ancestors, place, prior_states, targets.shape[0], seats)
    if paired:
        received = lax.ppermute(outgoing, "ens", swap)
    else:
        received = lax.all_to_all(outgoing, "ens", split_axis=0, concat_axis=0, tiled=True)
    log_weight = log_weights(prior_states, *rest[:-1])
    scaled, own_norm, own_mean, sent_mean = group_mean(
        log_weight, prior_states, chunk_of(heights)
    )
    if paired:
        other_norm = lax.ppermute(own_norm, "ens", swap)
        other_mean = lax.ppermute(sent_mean, "ens", swap)
    else:
        peak = lax.pmax(own_norm[0], "ens")
        part = own_norm[1] * jnp.exp(own_norm[0] - peak)
        total, own_mean = lax.psum((part, expand_patches(part)[None] * own_mean), "ens")
        own_mean = own_mean / expand_patches(total)[None]
        other_norm = jnp.stack([peak, total])
        other_mean = sent_mean
    return combine(
        ancestors,
        place,
        scaled,
        own_norm,
        other_norm,
        own_mean,
        other_mean,
        prior_states,
        received,
        chunk_of(heights),
        not paired,
    )


def solution(mesh):
    return jax.shard_map(
        body,
        mesh=mesh,
        in_specs=(
            P("ens", None, "lat", "lon"),
            P(None, "lat", "lon"),
            P("lat", "lon"),
            P(),
            P(),
            P(),
            P(),
            P(),
            P(),
            P(),
            P(None, "lat", "lon"),
        ),
        out_specs=(P("ens", None, "lat", "lon"), P("ens", "lat", "lon")),
        check_vma=False,
    )
```

```python
import jax
import jax.numpy as jnp
from jax import lax
from jax.experimental import pallas as pl
from jax.experimental.pallas import tpu as pltpu
from jax.sharding import PartitionSpec as P
import numpy as np

PATCH_NORTHWARD = 32
PATCH_EASTWARD = 128
RADIUS = 16


relax_factor = 0.6
PIECES = 4


def extended(shard, sides, width):
    for axis, dim in sides:
        peers, length = (lax.axis_size(axis), shard.shape[dim])
        up = [(i, (i + 1) % peers) for i in range(peers - 1)]
        down = [(j, i) for i, j in up]
        last = lax.slice_in_dim(shard, length - width, length, axis=dim)
        first = lax.slice_in_dim(shard, 0, width, axis=dim)
        before = lax.ppermute(last, axis, up)
        after = lax.ppermute(first, axis, down)
        shard = jnp.concatenate([before, shard, after], axis=dim)
    return shard


def taper_band(inner_count, radius):
    tap_count = 2 * radius + 1
    tap_width = radius / 2.0
    taps = np.exp(-0.5 * ((np.arange(tap_count) - radius) / tap_width) ** 2)
    taps = taps / taps.sum()
    band = np.zeros((inner_count, inner_count + 2 * radius), np.float32)
    for out_index in range(inner_count):
        band[out_index, out_index : out_index + tap_count] = taps
    return band


def expand_patches(values):
    lead = values.shape[:-2]
    rows, cols = (values.shape[-2], values.shape[-1])
    grown = jnp.broadcast_to(values[..., :, None, :, None], lead + (rows, 2, cols, 2))
    return grown.reshape(lead + (rows * 2, cols * 2))


LANES = 128


def store_doubled(out, values):
    count, rows, cols = values.shape
    of_cols = lax.broadcasted_iota(jnp.int32, (cols, 2 * cols), 0)
    to_cols = lax.broadcasted_iota(jnp.int32, (cols, 2 * cols), 1)
    wide = (lax.shift_right_logical(to_cols, 1) == of_cols).astype(jnp.float32)
    wide = wide.astype(jnp.bfloat16)
    rest = values.reshape(count * rows, cols)
    grown = None
    for _ in range(3):
        part = rest.astype(jnp.bfloat16)
        rest = rest - part.astype(jnp.float32)
        moved = jnp.dot(part, wide, preferred_element_type=jnp.float32)
        grown = moved if grown is None else grown + moved
    for which in range(count):
        for block in range(2 * cols // LANES):
            piece = grown[which * rows : (which + 1) * rows, block * LANES : (block + 1) * LANES]
            for half in range(2):
                out[which, block, pl.ds(half, rows, stride=2), :] = piece


def tiles_of(rows, cols):
    return [
        (north, east)
        for north in range(rows // PATCH_NORTHWARD)
        for east in range(cols // PATCH_EASTWARD)
    ]


def tile_window(north, east):
    return (
        pl.ds(north * PATCH_NORTHWARD, PATCH_NORTHWARD),
        pl.ds(east * PATCH_EASTWARD, PATCH_EASTWARD),
    )


def group_mean(borders, smooth, from_west, from_east, band, prior_states, pieces, chunk):
    members, pixel_rows, pixel_cols = smooth.shape
    _, heights, rows, cols = prior_states.shape
    blocks = cols // LANES
    per_piece = heights // chunk // pieces

    def kernel(border, own_ref, left, right, band_ref, prior, scaled_ref, norm_ref, mean_ref, *refs):
        sent, share = refs[:pieces], refs[pieces]
        step = pl.program_id(0)

        @pl.when(step == 0)
        def _():
            west = jnp.where(border[2] == 0, 0.0, left[...])
            east = jnp.where(border[3] == 0, 0.0, right[...])
            padded = jnp.concatenate([west, own_ref[...], east], axis=2)
            tapered = jnp.dot(
                padded.reshape(members * pixel_rows, 3 * pixel_cols),
                band_ref[...],
                precision=lax.Precision.HIGHEST,
            )
            values = -0.5 * tapered.reshape(members, pixel_rows, pixel_cols)
            peak = jnp.max(values, axis=0)
            scaled = jnp.exp(values - peak[None])
            total = jnp.sum(scaled, axis=0)
            scaled_ref[...] = scaled
            norm_ref[0] = peak
            norm_ref[1] = total
            store_doubled(share, scaled / total[None])

        for block in range(blocks):
            window = slice(block * LANES, (block + 1) * LANES)
            for level in range(chunk):
                mean = share[0, block] * prior[0, level, :, window].astype(jnp.float32)
                for member in range(1, members):
                    mean = mean + share[member, block] * prior[member, level, :, window].astype(
                        jnp.float32
                    )
                mean_ref[level, :, window] = mean
        for piece in range(pieces):

            @pl.when((step >= piece * per_piece) & (step < (piece + 1) * per_piece))
            def _(piece=piece):
                sent[piece][...] = mean_ref[...].astype(jnp.bfloat16)

    def whole(shape):
        return pl.BlockSpec(shape, lambda i, n=len(shape): (0,) * n)

    def piece_spec(piece):
        return pl.BlockSpec(
            (chunk, rows, cols),
            lambda i: (jnp.clip(i - piece * per_piece, 0, per_piece - 1), 0, 0),
        )

    norm = (2, pixel_rows, pixel_cols)
    return pl.pallas_call(
        kernel,
        grid=(heights // chunk,),
        out_shape=(
            jax.ShapeDtypeStruct(smooth.shape, jnp.float32),
            jax.ShapeDtypeStruct(norm, jnp.float32),
            jax.ShapeDtypeStruct((heights, rows, cols), jnp.float32),
        )
        + (jax.ShapeDtypeStruct((heights // pieces, rows, cols), jnp.bfloat16),) * pieces,
        in_specs=[
            pl.BlockSpec(memory_space=pltpu.SMEM),
            whole(smooth.shape),
            whole(smooth.shape),
            whole(smooth.shape),
            whole(band.shape),
            pl.BlockSpec((members, chunk, rows, cols), lambda i: (0, i, 0, 0)),
        ],
        out_specs=(
            whole(smooth.shape),
            whole(norm),
            pl.BlockSpec((chunk, rows, cols), lambda i: (i, 0, 0)),
        )
        + tuple(piece_spec(piece) for piece in range(pieces)),
        scratch_shapes=[pltpu.VMEM((members, blocks, rows, LANES), jnp.float32)],
        compiler_params=pltpu.CompilerParams(vmem_limit_bytes=16 << 20),
        name="group_mean",
    )(borders, smooth, from_west, from_east, band, prior_states)


def merge(scaled, own_norm, other_norm, shared):
    _, pixel_rows, pixel_cols = scaled.shape

    def kernel(scaled_ref, own_ref, other_ref, weights, parts):
        own_peak, own_total = own_ref[0], own_ref[1]
        other_peak, other_total = other_ref[0], other_ref[1]
        peak = jnp.maximum(own_peak, other_peak)
        own_scale = jnp.exp(own_peak - peak)
        own_part = own_total * own_scale
        if shared:
            total = other_total
            weighted = jnp.stack([jnp.ones_like(total), jnp.zeros_like(total)])
        else:
            other_part = other_total * jnp.exp(other_peak - peak)
            total = own_part + other_part
            weighted = jnp.stack([own_part, other_part]) / total[None]
        store_doubled(parts, (1.0 - relax_factor) * weighted)
        weights[...] = scaled_ref[...] * (own_scale / total)[None]

    return pl.pallas_call(
        kernel,
        out_shape=(
            jax.ShapeDtypeStruct(scaled.shape, jnp.float32),
            jax.ShapeDtypeStruct((2, 2 * pixel_cols // LANES, 2 * pixel_rows, LANES), jnp.float32),
        ),
        name="merge",
    )(scaled, own_norm, other_norm)


def combine(table, parts, own_mean, other_mean, prior_states, received, analysis, first, chunk):
    members, heights, rows, cols = prior_states.shape
    tiles = tiles_of(rows, cols)
    count = len(tiles)
    sources, seats = received.shape[:2]
    received = received.reshape((sources * seats,) + received.shape[2:])
    steps = other_mean.shape[0] // chunk
    start = first // chunk
    done = () if analysis is None else (analysis,)

    def kernel(lookup, parts_ref, mean_ref, peer_ref, prior, remote, *refs):
        out, base = refs[len(done) :]
        for block in range(cols // LANES):
            window = slice(block * LANES, (block + 1) * LANES)
            for level in range(chunk):
                base[level, :, window] = parts_ref[0, block] * mean_ref[
                    level, :, window
                ] + parts_ref[1, block] * peer_ref[level, :, window].astype(jnp.float32)

        def fill(array, source, slot, tile):
            north, east = tiles[tile]
            down = slice(north * PATCH_NORTHWARD, (north + 1) * PATCH_NORTHWARD)
            along = slice(east * PATCH_EASTWARD, (east + 1) * PATCH_EASTWARD)
            for level in range(chunk):
                out[slot, level, down, along] = base[level, down, along] + relax_factor * array[
                    source, level, down, along
                ].astype(jnp.float32)

        for slot in range(members):
            for tile in range(count):
                source = lookup[slot * count + tile]

                @pl.when(source < members)
                def _(slot=slot, tile=tile, source=source):
                    fill(prior, source, slot, tile)

                @pl.when(source >= members)
                def _(slot=slot, tile=tile, source=source):
                    fill(remote, source - members, slot, tile)

    return pl.pallas_call(
        kernel,
        grid=(steps,),
        out_shape=jax.ShapeDtypeStruct(prior_states.shape, jnp.float32),
        in_specs=[
            pl.BlockSpec(memory_space=pltpu.SMEM),
            pl.BlockSpec(parts.shape, lambda i: (0, 0, 0, 0)),
            pl.BlockSpec((chunk, rows, cols), lambda i: (start + i, 0, 0)),
            pl.BlockSpec((chunk, rows, cols), lambda i: (i, 0, 0)),
            pl.BlockSpec((members, chunk, rows, cols), lambda i: (0, start + i, 0, 0)),
            pl.BlockSpec((sources * seats, chunk, rows, cols), lambda i: (0, start + i, 0, 0)),
        ]
        + [pl.BlockSpec(memory_space=pltpu.HBM)] * len(done),
        out_specs=pl.BlockSpec((members, chunk, rows, cols), lambda i: (0, start + i, 0, 0)),
        input_output_aliases={6: 0} if done else {},
        scratch_shapes=[pltpu.VMEM((chunk, rows, cols), jnp.float32)],
        compiler_params=pltpu.CompilerParams(vmem_limit_bytes=24 << 20),
        name="combine",
    )(table, parts, own_mean, other_mean, prior_states, received, *done)


SLOTS = 3


def entry_layer(ancestors, place, prior_states, even_taps, odd_taps, targets, seats):
    members, heights, rows, cols = prior_states.shape
    tiles = tiles_of(rows, cols)
    count = len(tiles)
    groups = ancestors.shape[0] // (members * count)
    channels = odd_taps.shape[0] // 2
    padded = even_taps.shape[1] // 5
    pixel_rows, pixel_cols = rows // 2, cols // 2

    def kernel(
        ancestor, spot, prior, even_ref, odd_ref, field, out, east_ref, west_ref, picked, table,
        sorted_cells, lines, east, west, buffer, used, seen, sems,
    ):
        def transfer(target, seat, member, tile, leaving):
            window = tile_window(*tiles[tile])
            here = buffer.at[(target, seat, slice(None)) + window]
            sem = sems.at[int(leaving), target, seat, tile]
            if leaving:
                away = picked.at[(target, seat, slice(None)) + window]
                return pltpu.make_async_copy(here, away, sem)
            return pltpu.make_async_copy(field.at[(member, slice(None)) + window], here, sem)

        def each_seat(action):
            for target in range(targets):
                for tile in range(count):
                    for seat in range(seats):

                        @pl.when(seat < used[target * count + tile])
                        def _(target=target, tile=tile, seat=seat):
                            action(target, seat, tile)

        def load_then_send(target, seat, tile):
            transfer(target, seat, 0, tile, False).wait()
            transfer(target, seat, 0, tile, True).start()

        @pl.when(pl.program_id(0) == 0)
        def _():
            own = spot[0]
            for target in range(targets):
                for tile in range(count):
                    rank = jnp.int32(0)
                    for slot in range(members):
                        parent = ancestor[(spot[1 + target] * members + slot) * count + tile]
                        local = parent - own * members
                        hit = (local >= 0) & (local < members) & (rank < seats)

                        @pl.when(hit)
                        def _(target=target, rank=rank, local=local, tile=tile):
                            transfer(target, rank, local, tile, False).start()

                        rank = rank + hit.astype(jnp.int32)
                    used[target * count + tile] = rank
            for tile in range(count):
                for group in range(groups):
                    seen[group] = 0
                for slot in range(members):
                    parent = ancestor[(own * members + slot) * count + tile]
                    group = lax.div(parent, jnp.int32(members))
                    rank = seen[group]
                    seen[group] = rank + 1
                    line = (jnp.int32(0) if targets == 1 else group) * seats + rank
                    table[slot * count + tile] = jnp.where(
                        group == own, parent - own * members, members + line
                    )
            lines[...] = jnp.zeros_like(lines)

        @pl.when(pl.program_id(0) == members // 2)
        def _():
            each_seat(load_then_send)

        @pl.when(pl.program_id(0) == members - 1)
        def _():
            each_seat(lambda target, seat, tile: transfer(target, seat, 0, tile, True).wait())

        here = lax.broadcasted_iota(jnp.int32, (cols, cols), 0)
        there = lax.broadcasted_iota(jnp.int32, (cols, cols), 1)
        chosen = jnp.where(there < pixel_cols, 2 * there, 2 * (there - pixel_cols) + 1)
        parity = (here == chosen).astype(jnp.float32).astype(jnp.bfloat16)
        split = jnp.dot(
            prior[0].reshape(heights * rows, cols), parity, preferred_element_type=jnp.float32
        )
        for kind in range(2):
            sorted_cells[kind] = split[:, kind * pixel_cols : (kind + 1) * pixel_cols]
        for kind in range(2):
            for row in range(rows):
                lines[kind, row + 4, :heights] = sorted_cells[
                    kind, pl.ds(row, heights, stride=rows), :
                ].astype(jnp.bfloat16)
        east[...] = jnp.zeros_like(east)
        west[...] = jnp.zeros_like(west)
        lane = lax.broadcasted_iota(jnp.int32, (channels, pixel_cols), 1)
        last = pixel_cols - 1

        def window(kind, row):
            return lines[kind, 2 * row + 2 : 2 * row + 7].reshape(5 * padded, pixel_cols)

        for pair in range(-1, pixel_rows + 1, 2):
            even, odd = (
                jnp.dot(
                    taps[...],
                    jnp.concatenate([window(kind, pair), window(kind, pair + 1)], axis=1),
                    preferred_element_type=jnp.float32,
                )
                for kind, taps in ((0, even_ref), (1, odd_ref))
            )
            for half in range(2):
                row = pair + half
                here_even = even[:, half * pixel_cols : (half + 1) * pixel_cols]
                here_odd = odd[:, half * pixel_cols : (half + 1) * pixel_cols]
                ahead = pltpu.roll(here_even[:channels] + here_odd[:channels], 1, 1)
                behind = pltpu.roll(here_even[2 * channels :], last, 1)
                inside = (
                    here_even[channels : 2 * channels]
                    + here_odd[channels:]
                    + jnp.where(lane == 0, 0.0, ahead)
                    + jnp.where(lane == last, 0.0, behind)
                )
                out[0, row + 1] = inside
                at = 3 * (row + 2)
                onward = pltpu.roll(jnp.where(lane == 0, ahead, inside), at + 2, 1)
                east[...] = jnp.where((lane >= at) & (lane < at + 3), onward, east[...])
                onward = pltpu.roll(jnp.where(lane == last, behind, inside), 65 + at, 1)
                west[...] = jnp.where((lane >= 64 + at) & (lane < 67 + at), onward, west[...])
        east_ref[0] = east[...].astype(jnp.bfloat16)
        west_ref[0] = west[...].astype(jnp.bfloat16)

    sent = (targets, seats, heights, rows, cols)
    edge = jax.ShapeDtypeStruct((members, channels, pixel_cols), jnp.bfloat16)
    edge_spec = pl.BlockSpec((1, channels, pixel_cols), lambda i: (i, 0, 0))
    return pl.pallas_call(
        kernel,
        grid=(members,),
        out_shape=(
            pltpu.HBM((members, pixel_rows + 2, channels, pixel_cols), jnp.float32),
            edge,
            edge,
            jax.ShapeDtypeStruct(sent, prior_states.dtype),
            jax.ShapeDtypeStruct((members * count,), jnp.int32),
        ),
        in_specs=[
            pl.BlockSpec(memory_space=pltpu.SMEM),
            pl.BlockSpec(memory_space=pltpu.SMEM),
            pl.BlockSpec((1, heights, rows, cols), lambda i: (i, 0, 0, 0)),
            pl.BlockSpec(even_taps.shape, lambda i: (0, 0)),
            pl.BlockSpec(odd_taps.shape, lambda i: (0, 0)),
            pl.BlockSpec(memory_space=pltpu.HBM),
        ],
        out_specs=(
            pl.BlockSpec((1, pixel_rows + 2, channels, pixel_cols), lambda i: (i, 0, 0, 0)),
            edge_spec,
            edge_spec,
            pl.BlockSpec(memory_space=pltpu.HBM),
            pl.BlockSpec(memory_space=pltpu.SMEM),
        ),
        scratch_shapes=[
            pltpu.VMEM((2, heights * rows, pixel_cols), jnp.float32),
            pltpu.VMEM((2, rows + 8, padded, pixel_cols), jnp.bfloat16),
            pltpu.VMEM((channels, pixel_cols), jnp.float32),
            pltpu.VMEM((channels, pixel_cols), jnp.float32),
            pltpu.VMEM(sent, prior_states.dtype),
            pltpu.SMEM((targets * count,), jnp.int32),
            pltpu.SMEM((groups,), jnp.int32),
            pltpu.SemaphoreType.DMA((2, targets, seats, count)),
        ],
        compiler_params=pltpu.CompilerParams(vmem_limit_bytes=28 << 20),
        name="entry_layer",
    )(ancestors, place, prior_states, even_taps, odd_taps, prior_states)


def received_sides(from_west, from_east, border):
    west = jnp.where(border[2] == 0, 0.0, from_west.astype(jnp.float32))
    east = jnp.where(border[3] == 0, 0.0, from_east.astype(jnp.float32))
    return west, east


def end_fix(west, east, lane):
    return jnp.where(lax.rem(lane, 3) == 2, west, pltpu.roll(east, 65, 1))


def with_ends(values, fix, row, lane):
    moved = pltpu.roll(fix, (128 - 3 * (row + 2) - 2) % 128, 1)
    return values + jnp.where((lane == 0) | (lane == 127), moved, 0.0)


def side_columns(west, east, own_east, own_west, lane):
    spill = jnp.where(
        lane < 64,
        pltpu.roll(own_west.astype(jnp.float32), 65, 1),
        pltpu.roll(own_east.astype(jnp.float32), 63, 1),
    )
    middle = lax.rem(lax.rem(lane, 64), 3) == 1
    return jnp.where(lane < 64, west, east) + jnp.where(middle, spill, 0.0)


def row_ends(borders, partial, own_east, own_west, from_west, from_east):
    members, row_count, channels, pixel_cols = partial.shape
    tail = row_count // SLOTS - 1

    def kernel(border, top, bottom, own_e, own_w, left, right, north, south):
        lane = lax.broadcasted_iota(jnp.int32, (channels, pixel_cols), 1)
        for member in range(members):
            west, east = received_sides(left[member], right[member], border)
            fix = end_fix(west, east, lane)
            sides = side_columns(west, east, own_e[member], own_w[member], lane)
            for slot in range(SLOTS):
                north[member, slot] = with_ends(top[member, slot], fix, slot - 1, lane).astype(
                    jnp.bfloat16
                )
                south[member, slot] = with_ends(
                    bottom[member, slot], fix, row_count - 4 + slot, lane
                ).astype(jnp.bfloat16)
            north[member, SLOTS] = sides.astype(jnp.bfloat16)
            south[member, SLOTS] = sides.astype(jnp.bfloat16)

    edge_spec = pl.BlockSpec((members, channels, pixel_cols), lambda i: (0, 0, 0))
    rows_spec = (members, SLOTS, channels, pixel_cols)
    sent = (members, SLOTS + 1, channels, pixel_cols)
    return pl.pallas_call(
        kernel,
        grid=(1,),
        out_shape=(jax.ShapeDtypeStruct(sent, jnp.bfloat16),) * 2,
        in_specs=[
            pl.BlockSpec(memory_space=pltpu.SMEM),
            pl.BlockSpec(rows_spec, lambda i: (0, 0, 0, 0)),
            pl.BlockSpec(rows_spec, lambda i: (0, tail, 0, 0)),
            edge_spec,
            edge_spec,
            edge_spec,
            edge_spec,
        ],
        out_specs=(pl.BlockSpec(sent, lambda i: (0, 0, 0, 0)),) * 2,
        compiler_params=pltpu.CompilerParams(vmem_limit_bytes=16 << 20),
        name="row_ends",
    )(borders, partial, partial, own_east, own_west, from_west, from_east)


def misfits(borders, partial, sides, rows_in, inner, fixed):
    members, row_count, channels, pixel_cols = partial.shape
    pixel_rows = row_count - 2
    bands = fixed[2].shape[0]
    edge = SLOTS
    whole_rows = rows_in is None
    if whole_rows:
        wanted = list(range(edge, pixel_rows - edge))
        needed = range(edge - 2, pixel_rows - edge + 2)
    else:
        wanted = [*range(edge), *range(pixel_rows - edge, pixel_rows)]
        needed = [*range(-2, edge + 2), *range(pixel_rows - edge - 2, pixel_rows + 2)]

    def kernel(*refs):
        border, pre, own_e, own_w, left, right = refs[:6]
        refs = refs[6:]
        if not whole_rows:
            above, below, inner_ref = refs[:3]
            refs = refs[3:]
        vectors, weight, matrix_ref, obs, mask_ref = refs[:5]
        out, hidden, taps, side = refs[5:]

        @pl.when(pl.program_id(0) == 0)
        def _():
            for down in range(3):
                line = slice(down * channels, (down + 1) * channels)
                for along in range(3):
                    part = weight[down, along]
                    taps[along * channels : (along + 1) * channels, line] = part
                    if along != 1:
                        half = along // 2 * channels
                        side[half : half + channels, line] = part

        lane = lax.broadcasted_iota(jnp.int32, (channels, pixel_cols), 1)
        bias = jnp.broadcast_to(vectors[:, 0:1], (channels, pixel_cols))
        bias_two = jnp.broadcast_to(vectors[:, 1:2], (channels, pixel_cols))
        offset = jnp.broadcast_to(vectors[:bands, 2:3], (bands, pixel_cols))
        variance = jnp.broadcast_to(vectors[:bands, 3:4], (bands, pixel_cols))
        top, bottom = border[0] == 0, border[1] == 0
        start, end = border[2] == 0, border[3] == 0
        west, east = received_sides(left[0], right[0], border)
        fix = end_fix(west, east, lane)

        for row in needed:
            if row == -2:
                values = above[0, 0].astype(jnp.float32)
            elif row == pixel_rows + 1:
                values = below[0, SLOTS - 1].astype(jnp.float32)
            else:
                values = with_ends(pre[0, row + 1], fix, row, lane)
                if row <= 0:
                    values = values + above[0, row + 2].astype(jnp.float32)
                if row >= pixel_rows - 1:
                    values = values + below[0, row - pixel_rows + 1].astype(jnp.float32)
            values = jnp.maximum(values + bias, 0.0)
            if row < 0:
                values = jnp.where(top, 0.0, values)
            if row >= pixel_rows:
                values = jnp.where(bottom, 0.0, values)
            hidden[row + 2] = values.astype(jnp.bfloat16)

        slot = lax.div(lax.rem(lane, 64), 3)
        cells = side_columns(west, east, own_e[0], own_w[0], lane)
        outside = (start & (lane < 64)) | (end & (lane >= 64))
        if not whole_rows:
            upper = pltpu.roll(above[0, SLOTS].astype(jnp.float32), 128 - 3 * pixel_rows, 1)
            lower = pltpu.roll(below[0, SLOTS].astype(jnp.float32), 3 * pixel_rows, 1)
            cells = (
                cells
                + jnp.where(slot < 3, upper, 0.0)
                + jnp.where((slot > pixel_rows) & (slot < pixel_rows + 4), lower, 0.0)
            )
            outside = outside | (top & (slot < 2)) | (bottom & (slot >= pixel_rows + 2))
        cells = jnp.where(outside, 0.0, jnp.maximum(cells + bias, 0.0))
        stack = jnp.concatenate(
            [pltpu.roll(cells, 6, 1), cells, pltpu.roll(cells, 122, 1)], axis=0
        ).astype(jnp.bfloat16)
        found = jnp.dot(side[...], stack, preferred_element_type=jnp.float32)
        column = jnp.where(lane < 64, found[:channels], found[channels:])

        def window(row):
            return jnp.concatenate([hidden[row], hidden[row + 2], hidden[row + 4]], axis=0)

        if not whole_rows:
            out[0, edge : pixel_rows - edge] = inner_ref[0, edge : pixel_rows - edge]
        for first, second in zip(wanted[::2], wanted[1::2]):
            both = jnp.dot(
                taps[...],
                jnp.concatenate([window(first), window(second)], axis=1),
                preferred_element_type=jnp.float32,
            )
            ready = []
            for half, row in enumerate((first, second)):
                parts = both[:, half * pixel_cols : (half + 1) * pixel_cols]
                at = 3 * (row + 2)
                values = (
                    parts[channels : 2 * channels]
                    + jnp.where(
                        lane < 2,
                        pltpu.roll(column, 128 - at, 1),
                        pltpu.roll(parts[:channels], 2, 1),
                    )
                    + jnp.where(
                        lane >= 126,
                        pltpu.roll(column, (189 - at) % 128, 1),
                        pltpu.roll(parts[2 * channels :], 126, 1),
                    )
                )
                ready.append(jnp.maximum(values + bias_two, 0.0).astype(jnp.bfloat16))
            predicted = jnp.dot(
                matrix_ref[...],
                jnp.concatenate(ready, axis=1),
                preferred_element_type=jnp.float32,
            )
            for half, row in enumerate((first, second)):
                misfit = obs[pl.ds(row, bands, stride=pixel_rows), :] - (
                    predicted[:, half * pixel_cols : (half + 1) * pixel_cols] + offset
                )
                total = jnp.sum(misfit * misfit / variance, axis=0, keepdims=True)
                out[0, row : row + 1] = total * mask_ref[row : row + 1].astype(jnp.float32)

    edge_spec = pl.BlockSpec((1, channels, pixel_cols), lambda i: (i, 0, 0))
    line_spec = pl.BlockSpec((1, SLOTS + 1, channels, pixel_cols), lambda i: (i, 0, 0, 0))
    out_spec = pl.BlockSpec((1, pixel_rows, pixel_cols), lambda i: (i, 0, 0))

    def whole(array):
        return pl.BlockSpec(array.shape, lambda i, n=array.ndim: (0,) * n)

    extra = () if whole_rows else (*rows_in, inner)
    extra_specs = [] if whole_rows else [line_spec, line_spec, out_spec]
    return pl.pallas_call(
        kernel,
        grid=(members,),
        out_shape=jax.ShapeDtypeStruct((members, pixel_rows, pixel_cols), jnp.float32),
        in_specs=[
            pl.BlockSpec(memory_space=pltpu.SMEM),
            pl.BlockSpec((1, row_count, channels, pixel_cols), lambda i: (i, 0, 0, 0)),
        ]
        + [edge_spec] * 4
        + extra_specs
        + [whole(array) for array in fixed],
        out_specs=out_spec,
        scratch_shapes=[
            pltpu.VMEM((pixel_rows + 4, channels, pixel_cols), jnp.bfloat16),
            pltpu.VMEM((3 * channels, 3 * channels), jnp.bfloat16),
            pltpu.VMEM((2 * channels, 3 * channels), jnp.bfloat16),
        ],
        compiler_params=pltpu.CompilerParams(vmem_limit_bytes=16 << 20),
        name="inner_misfits" if whole_rows else "outer_misfits",
    )(borders, partial, *sides, *extra, *fixed)


def neighbours(axis):
    count = lax.axis_size(axis)
    onward = [(i, i + 1) for i in range(count - 1)]
    return onward, [(j, i) for i, j in onward]


def departures(
    ancestors,
    place,
    targets,
    seats,
    prior_states,
    measured_brightness,
    measured_indicator,
    sensor_error_spread,
    entry_layer_stencil,
    entry_layer_offset,
    middle_layer_stencil,
    middle_layer_offset,
    brightness_matrix,
    brightness_offset,
):
    channels, heights = entry_layer_stencil.shape[:2]
    padded = (heights + 15) // 16 * 16
    entry = jnp.pad(entry_layer_stencil, ((0, 0), (0, padded - heights), (0, 0), (0, 0)))
    entry = jnp.transpose(entry, (3, 0, 2, 1)).reshape(5, channels, 5 * padded)
    even_taps = jnp.concatenate([entry[0], entry[2], entry[4]])
    odd_taps = jnp.concatenate([entry[1], entry[3]])
    lat, lon = lax.axis_index("lat"), lax.axis_index("lon")
    borders = jnp.stack(
        [lat, lax.axis_size("lat") - 1 - lat, lon, lax.axis_size("lon") - 1 - lon]
    ).astype(jnp.int32)
    partial, own_east, own_west, picked, table = entry_layer(
        ancestors,
        place,
        pltpu.with_memory_space_constraint(prior_states, pltpu.HBM),
        even_taps,
        odd_taps,
        targets,
        seats,
    )
    partial = pltpu.with_memory_space_constraint(partial, pltpu.HBM)
    count = lax.axis_size("lon")
    ring = [(i, (i + 1) % count) for i in range(count)]
    from_west = lax.ppermute(own_east, "lon", ring)
    from_east = lax.ppermute(own_west, "lon", [(j, i) for i, j in ring])
    sides = (own_east, own_west, from_west, from_east)
    north, south = row_ends(borders, partial, *sides)
    onward, back = neighbours("lat")
    from_north = lax.ppermute(south, "lat", onward)
    from_south = lax.ppermute(north, "lat", back)
    bands = brightness_matrix.shape[0]
    vectors = jnp.stack(
        [
            entry_layer_offset,
            middle_layer_offset,
            jnp.pad(brightness_offset, (0, channels - bands)),
            jnp.pad(sensor_error_spread, (0, channels - bands), constant_values=1.0),
        ],
        axis=1,
    )
    fixed = (
        vectors,
        jnp.transpose(middle_layer_stencil, (2, 3, 0, 1)),
        brightness_matrix,
        measured_brightness.reshape(-1, measured_brightness.shape[-1]),
        measured_indicator,
    )
    inner = misfits(borders, partial, sides, None, None, fixed)
    squares = misfits(borders, partial, sides, (from_north, from_south), inner, fixed)
    return squares, picked, table, borders


def chunk_of(heights):
    return next(size for size in (5, 4, 2, 1) if heights % size == 0)


def body(prior_states, *rest):
    ancestor_indices = rest[-1]
    members, heights, rows, cols = prior_states.shape
    groups = lax.axis_size("ens")
    own = lax.axis_index("ens").astype(jnp.int32)
    seats = max(2, (members + groups - 1) // groups)
    ancestors = ancestor_indices.reshape(-1)
    swap = [(0, 1), (1, 0)]
    paired = groups == 2
    if paired:
        targets = (1 - own)[None]
    else:
        targets = jnp.arange(groups, dtype=jnp.int32)
    place = jnp.concatenate([own[None], targets])
    squares, picked, table, borders = departures(
        ancestors, place, targets.shape[0], seats, prior_states, *rest[:-1]
    )
    if paired:
        received = lax.ppermute(picked, "ens", swap)
    else:
        received = lax.all_to_all(picked, "ens", split_axis=0, concat_axis=0, tiled=True)
    band_lat = taper_band(squares.shape[1], RADIUS)
    padded = extended(squares, (("lat", 1),), RADIUS)
    smooth = jnp.einsum("ij,pjk->pik", band_lat, padded, precision=lax.Precision.HIGHEST)
    pixel_cols = squares.shape[2]
    band_lon = np.zeros((3 * pixel_cols, pixel_cols), np.float32)
    near = slice(pixel_cols - RADIUS, 2 * pixel_cols + RADIUS)
    band_lon[near] = taper_band(pixel_cols, RADIUS).T
    count = lax.axis_size("lon")
    ring = [(i, (i + 1) % count) for i in range(count)]
    from_west = lax.ppermute(smooth, "lon", ring)
    from_east = lax.ppermute(smooth, "lon", [(j, i) for i, j in ring])
    size = chunk_of(heights)
    pieces = PIECES if heights // size % PIECES == 0 else 1
    levels = heights // pieces
    field = prior_states
    scaled, own_norm, own_mean, *sent = group_mean(
        borders, smooth, from_west, from_east, band_lon, field, pieces, size
    )
    if paired:
        other_norm = lax.ppermute(own_norm, "ens", swap)
        others = [lax.ppermute(piece, "ens", swap) for piece in sent]
    else:
        peak = lax.pmax(own_norm[0], "ens")
        part = own_norm[1] * jnp.exp(own_norm[0] - peak)
        total, added = lax.psum((part, expand_patches(part)[None] * own_mean), "ens")
        own_mean = added / expand_patches(total)[None]
        other_norm = jnp.stack([peak, total])
        others = sent
    weights, parts = merge(scaled, own_norm, other_norm, not paired)
    analysis = None
    for k, other_mean in enumerate(others):
        analysis = combine(
            table, parts, own_mean, other_mean, field, received, analysis, k * levels, size
        )
    return analysis, weights


def solution(mesh):
    return jax.shard_map(
        body,
        mesh=mesh,
        in_specs=(
            P("ens", None, "lat", "lon"),
            P(None, "lat", "lon"),
            P("lat", "lon"),
            P(),
            P(),
            P(),
            P(),
            P(),
            P(),
            P(),
            P(None, "lat", "lon"),
        ),
        out_specs=(P("ens", None, "lat", "lon"), P("ens", "lat", "lon")),
        check_vma=False,
    )
```

```python
import math

import jax
import jax.numpy as jnp
from jax import lax
from jax.experimental import pallas as pl
from jax.experimental.pallas import tpu as pltpu
from jax.sharding import PartitionSpec as P
import numpy as np

PATCH_NORTHWARD = 32
PATCH_EASTWARD = 128
RADIUS = 16


relax_factor = 0.6
PIECES = 4


def extended(shard, sides, width):
    for axis, dim in sides:
        peers, length = (lax.axis_size(axis), shard.shape[dim])
        up = [(i, (i + 1) % peers) for i in range(peers - 1)]
        down = [(j, i) for i, j in up]
        last = lax.slice_in_dim(shard, length - width, length, axis=dim)
        first = lax.slice_in_dim(shard, 0, width, axis=dim)
        before = lax.ppermute(last, axis, up)
        after = lax.ppermute(first, axis, down)
        shard = jnp.concatenate([before, shard, after], axis=dim)
    return shard


def taper_band(inner_count, radius):
    tap_count = 2 * radius + 1
    tap_width = radius / 2.0
    taps = np.exp(-0.5 * ((np.arange(tap_count) - radius) / tap_width) ** 2)
    taps = taps / taps.sum()
    band = np.zeros((inner_count, inner_count + 2 * radius), np.float32)
    for out_index in range(inner_count):
        band[out_index, out_index : out_index + tap_count] = taps
    return band


def expand_patches(values):
    lead = values.shape[:-2]
    rows, cols = (values.shape[-2], values.shape[-1])
    grown = jnp.broadcast_to(values[..., :, None, :, None], lead + (rows, 2, cols, 2))
    return grown.reshape(lead + (rows * 2, cols * 2))


LANES = 128


def held(array):
    return pltpu.with_memory_space_constraint(array, pltpu.HBM)


def store_doubled(out, values):
    count, rows, cols = values.shape
    of_cols = lax.broadcasted_iota(jnp.int32, (cols, 2 * cols), 0)
    to_cols = lax.broadcasted_iota(jnp.int32, (cols, 2 * cols), 1)
    wide = (lax.shift_right_logical(to_cols, 1) == of_cols).astype(jnp.float32)
    wide = wide.astype(jnp.bfloat16)
    rest = values.reshape(count * rows, cols)
    grown = None
    for _ in range(3):
        part = rest.astype(jnp.bfloat16)
        rest = rest - part.astype(jnp.float32)
        moved = jnp.dot(part, wide, preferred_element_type=jnp.float32)
        grown = moved if grown is None else grown + moved
    for which in range(count):
        for block in range(2 * cols // LANES):
            piece = grown[which * rows : (which + 1) * rows, block * LANES : (block + 1) * LANES]
            for half in range(2):
                out[which, block, pl.ds(half, rows, stride=2), :] = piece


def tiles_of(rows, cols):
    return [
        (north, east)
        for north in range(rows // PATCH_NORTHWARD)
        for east in range(cols // PATCH_EASTWARD)
    ]


def tile_window(north, east):
    return (
        pl.ds(north * PATCH_NORTHWARD, PATCH_NORTHWARD),
        pl.ds(east * PATCH_EASTWARD, PATCH_EASTWARD),
    )


def group_mean(borders, smooth, from_west, from_east, band, prior_states, pieces, chunk):
    members, pixel_rows, pixel_cols = smooth.shape
    _, heights, rows, cols = prior_states.shape
    blocks = cols // LANES
    per_piece = heights // chunk // pieces

    def kernel(border, own_ref, left, right, band_ref, prior, scaled_ref, norm_ref, mean_ref, *refs):
        sent, share = refs[:pieces], refs[pieces]
        step = pl.program_id(0)

        @pl.when(step == 0)
        def _():
            west = jnp.where(border[2] == 0, 0.0, left[...])
            east = jnp.where(border[3] == 0, 0.0, right[...])
            padded = jnp.concatenate([west, own_ref[...], east], axis=2)
            tapered = jnp.dot(
                padded.reshape(members * pixel_rows, 3 * pixel_cols),
                band_ref[...],
                precision=lax.Precision.HIGHEST,
            )
            values = -0.5 * tapered.reshape(members, pixel_rows, pixel_cols)
            peak = jnp.max(values, axis=0)
            scaled = jnp.exp(values - peak[None])
            total = jnp.sum(scaled, axis=0)
            scaled_ref[...] = scaled
            norm_ref[0] = peak
            norm_ref[1] = total
            store_doubled(share, scaled / total[None])

        for block in range(blocks):
            window = slice(block * LANES, (block + 1) * LANES)
            for level in range(chunk):
                mean = share[0, block] * prior[0, level, :, window].astype(jnp.float32)
                for member in range(1, members):
                    mean = mean + share[member, block] * prior[member, level, :, window].astype(
                        jnp.float32
                    )
                mean_ref[level, :, window] = mean
        for piece in range(pieces):

            @pl.when((step >= piece * per_piece) & (step < (piece + 1) * per_piece))
            def _(piece=piece):
                sent[piece][...] = mean_ref[...].astype(jnp.bfloat16)

    def whole(shape):
        return pl.BlockSpec(shape, lambda i, n=len(shape): (0,) * n)

    def piece_spec(piece):
        return pl.BlockSpec(
            (chunk, rows, cols),
            lambda i: (jnp.clip(i - piece * per_piece, 0, per_piece - 1), 0, 0),
        )

    norm = (2, pixel_rows, pixel_cols)
    return pl.pallas_call(
        kernel,
        grid=(heights // chunk,),
        out_shape=(
            pltpu.HBM(smooth.shape, jnp.float32),
            pltpu.HBM(norm, jnp.float32),
            jax.ShapeDtypeStruct((heights, rows, cols), jnp.float32),
        )
        + (jax.ShapeDtypeStruct((heights // pieces, rows, cols), jnp.bfloat16),) * pieces,
        in_specs=[
            pl.BlockSpec(memory_space=pltpu.SMEM),
            whole(smooth.shape),
            whole(smooth.shape),
            whole(smooth.shape),
            whole(band.shape),
            pl.BlockSpec((members, chunk, rows, cols), lambda i: (0, i, 0, 0)),
        ],
        out_specs=(
            whole(smooth.shape),
            whole(norm),
            pl.BlockSpec((chunk, rows, cols), lambda i: (i, 0, 0)),
        )
        + tuple(piece_spec(piece) for piece in range(pieces)),
        scratch_shapes=[pltpu.VMEM((members, blocks, rows, LANES), jnp.float32)],
        compiler_params=pltpu.CompilerParams(vmem_limit_bytes=16 << 20),
        name="group_mean",
    )(borders, smooth, from_west, from_east, band, prior_states)


def merge(scaled, own_norm, other_norm, shared):
    _, pixel_rows, pixel_cols = scaled.shape

    def kernel(scaled_ref, own_ref, other_ref, weights, parts):
        own_peak, own_total = own_ref[0], own_ref[1]
        other_peak, other_total = other_ref[0], other_ref[1]
        peak = jnp.maximum(own_peak, other_peak)
        own_scale = jnp.exp(own_peak - peak)
        own_part = own_total * own_scale
        if shared:
            total = other_total
            weighted = jnp.stack([jnp.ones_like(total), jnp.zeros_like(total)])
        else:
            other_part = other_total * jnp.exp(other_peak - peak)
            total = own_part + other_part
            weighted = jnp.stack([own_part, other_part]) / total[None]
        store_doubled(parts, (1.0 - relax_factor) * weighted)
        weights[...] = scaled_ref[...] * (own_scale / total)[None]

    return pl.pallas_call(
        kernel,
        out_shape=(
            jax.ShapeDtypeStruct(scaled.shape, jnp.float32),
            pltpu.HBM((2, 2 * pixel_cols // LANES, 2 * pixel_rows, LANES), jnp.float32),
        ),
        name="merge",
    )(held(scaled), held(own_norm), other_norm)


def combine(table, parts, own_mean, other_mean, prior_states, received, analysis, first, chunk):
    members, heights, rows, cols = prior_states.shape
    tiles = tiles_of(rows, cols)
    count = len(tiles)
    sources, seats = received.shape[:2]
    received = received.reshape((sources * seats,) + received.shape[2:])
    steps = other_mean.shape[0] // chunk
    start = first // chunk
    done = () if analysis is None else (analysis,)

    def kernel(lookup, parts_ref, mean_ref, peer_ref, prior, remote, *refs):
        analysis_ref, out, base, sems = refs[len(done) :]
        step = pl.program_id(0)
        half = lax.rem(step, 2)

        def leave(at, slot, which):
            return pltpu.make_async_copy(
                out.at[which, slot],
                analysis_ref.at[slot, pl.ds(first + at * chunk, chunk)],
                sems.at[which, slot],
            )

        for block in range(cols // LANES):
            window = slice(block * LANES, (block + 1) * LANES)
            for level in range(chunk):
                base[level, :, window] = parts_ref[0, block] * mean_ref[
                    level, :, window
                ] + parts_ref[1, block] * peer_ref[level, :, window].astype(jnp.float32)

        def fill(array, source, slot, tile):
            north, east = tiles[tile]
            down = slice(north * PATCH_NORTHWARD, (north + 1) * PATCH_NORTHWARD)
            along = slice(east * PATCH_EASTWARD, (east + 1) * PATCH_EASTWARD)
            for level in range(chunk):
                out[half, slot, level, down, along] = base[level, down, along] + relax_factor * array[
                    source, level, down, along
                ].astype(jnp.float32)

        for slot in range(members):

            @pl.when(step >= 2)
            def _(slot=slot):
                leave(step - 2, slot, half).wait()

            for tile in range(count):
                source = lookup[slot * count + tile]

                @pl.when(source < members)
                def _(slot=slot, tile=tile, source=source):
                    fill(prior, source, slot, tile)

                @pl.when(source >= members)
                def _(slot=slot, tile=tile, source=source):
                    fill(remote, source - members, slot, tile)

            leave(step, slot, half).start()

        @pl.when(step == steps - 1)
        def _():
            for slot in range(members):
                if steps > 1:
                    leave(step - 1, slot, 1 - half).wait()
                leave(step, slot, half).wait()

    return pl.pallas_call(
        kernel,
        grid=(steps,),
        out_shape=jax.ShapeDtypeStruct(prior_states.shape, jnp.float32),
        in_specs=[
            pl.BlockSpec(memory_space=pltpu.SMEM),
            pl.BlockSpec(parts.shape, lambda i: (0, 0, 0, 0)),
            pl.BlockSpec((chunk, rows, cols), lambda i: (start + i, 0, 0)),
            pl.BlockSpec((chunk, rows, cols), lambda i: (i, 0, 0)),
            pl.BlockSpec((members, chunk, rows, cols), lambda i: (0, start + i, 0, 0)),
            pl.BlockSpec((sources * seats, chunk, rows, cols), lambda i: (0, start + i, 0, 0)),
        ]
        + [pl.BlockSpec(memory_space=pltpu.HBM)] * len(done),
        out_specs=pl.BlockSpec(memory_space=pltpu.HBM),
        input_output_aliases={6: 0} if done else {},
        scratch_shapes=[
            pltpu.VMEM((2, members, chunk, rows, cols), jnp.float32),
            pltpu.VMEM((chunk, rows, cols), jnp.float32),
            pltpu.SemaphoreType.DMA((2, members)),
        ],
        compiler_params=pltpu.CompilerParams(vmem_limit_bytes=12 << 20),
        name="combine",
    )(table, held(parts), own_mean, other_mean, held(prior_states), held(received), *done)


SLOTS = 3
PACKED = 4


def entry_layer(ancestors, place, prior_states, weights, targets, seats):
    members, heights, rows, cols = prior_states.shape
    tiles = tiles_of(rows, cols)
    count = len(tiles)
    groups = ancestors.shape[1] // members
    channels = weights.shape[-1]
    padded = pl.cdiv(heights, 16) * 16
    pixel_rows, pixel_cols = rows // 2, cols // 2

    def kernel(
        ancestor, spot, prior, weight, field, out, east_ref, west_ref, picked, table,
        sorted_cells, lines, even_ref, odd_ref, east, west, buffer, used, seen, sems,
    ):
        def transfer(target, seat, member, tile, leaving):
            window = tile_window(*tiles[tile])
            here = buffer.at[(target, seat, slice(None)) + window]
            sem = sems.at[int(leaving), target, seat, tile]
            if leaving:
                away = picked.at[(target, seat, slice(None)) + window]
                return pltpu.make_async_copy(here, away, sem)
            return pltpu.make_async_copy(field.at[(member, slice(None)) + window], here, sem)

        def each_seat(action):
            for target in range(targets):
                for tile in range(count):
                    for seat in range(seats):

                        @pl.when(seat < used[target * count + tile])
                        def _(target=target, tile=tile, seat=seat):
                            action(target, seat, tile)

        def load_then_send(target, seat, tile):
            transfer(target, seat, 0, tile, False).wait()
            transfer(target, seat, 0, tile, True).start()

        @pl.when(pl.program_id(0) == 0)
        def _():
            own = spot[0]
            for target in range(targets):
                for tile in range(count):
                    rank = jnp.int32(0)
                    for slot in range(members):
                        parent = ancestor[tile, spot[1 + target] * members + slot]
                        local = parent - own * members
                        hit = (local >= 0) & (local < members) & (rank < seats)

                        @pl.when(hit)
                        def _(target=target, rank=rank, local=local, tile=tile):
                            transfer(target, rank, local, tile, False).start()

                        rank = rank + hit.astype(jnp.int32)
                    used[target * count + tile] = rank
            for tile in range(count):
                for group in range(groups):
                    seen[group] = 0
                for slot in range(members):
                    parent = ancestor[tile, own * members + slot]
                    group = lax.div(parent, jnp.int32(members))
                    rank = seen[group]
                    seen[group] = rank + 1
                    line = (jnp.int32(0) if targets == 1 else group) * seats + rank
                    table[slot * count + tile] = jnp.where(
                        group == own, parent - own * members, members + line
                    )
            lines[...] = jnp.zeros_like(lines)
            even_ref[...] = jnp.zeros_like(even_ref)
            odd_ref[...] = jnp.zeros_like(odd_ref)
            for down in range(5):
                for along in range(5):
                    part = weight[down, along].astype(jnp.float32).T.astype(jnp.bfloat16)
                    taps = odd_ref if along % 2 else even_ref
                    line = along // 2 * channels
                    taps[line : line + channels, down * padded : down * padded + heights] = part

        @pl.when(pl.program_id(0) == members // 2)
        def _():
            each_seat(load_then_send)

        @pl.when(pl.program_id(0) == members - 1)
        def _():
            each_seat(lambda target, seat, tile: transfer(target, seat, 0, tile, True).wait())

        here = lax.broadcasted_iota(jnp.int32, (cols, cols), 0)
        there = lax.broadcasted_iota(jnp.int32, (cols, cols), 1)
        chosen = jnp.where(there < pixel_cols, 2 * there, 2 * (there - pixel_cols) + 1)
        parity = (here == chosen).astype(jnp.float32).astype(jnp.bfloat16)
        split = jnp.dot(
            prior[0].reshape(heights * rows, cols), parity, preferred_element_type=jnp.float32
        )
        for kind in range(2):
            sorted_cells[kind] = split[:, kind * pixel_cols : (kind + 1) * pixel_cols]
        for kind in range(2):
            for row in range(rows):
                lines[kind, row + 4, :heights] = sorted_cells[
                    kind, pl.ds(row, heights, stride=rows), :
                ].astype(jnp.bfloat16)
        east[...] = jnp.zeros_like(east)
        west[...] = jnp.zeros_like(west)
        lane = lax.broadcasted_iota(jnp.int32, (channels, pixel_cols), 1)
        last = pixel_cols - 1

        def window(kind, row):
            return lines[kind, 2 * row + 2 : 2 * row + 7].reshape(5 * padded, pixel_cols)

        for pair in range(-1, pixel_rows + 1, 2):
            even, odd = (
                jnp.dot(
                    taps[...],
                    jnp.concatenate([window(kind, pair), window(kind, pair + 1)], axis=1),
                    preferred_element_type=jnp.float32,
                )
                for kind, taps in ((0, even_ref), (1, odd_ref))
            )
            for half in range(2):
                row = pair + half
                here_even = even[:, half * pixel_cols : (half + 1) * pixel_cols]
                here_odd = odd[:, half * pixel_cols : (half + 1) * pixel_cols]
                ahead = pltpu.roll(here_even[:channels] + here_odd[:channels], 1, 1)
                behind = pltpu.roll(here_even[2 * channels :], last, 1)
                inside = (
                    here_even[channels : 2 * channels]
                    + here_odd[channels:]
                    + jnp.where(lane == 0, 0.0, ahead)
                    + jnp.where(lane == last, 0.0, behind)
                )
                out[0, row + 1] = inside
                at = 3 * (row + 2)
                onward = pltpu.roll(jnp.where(lane == 0, ahead, inside), at + 2, 1)
                east[...] = jnp.where((lane >= at) & (lane < at + 3), onward, east[...])
                onward = pltpu.roll(jnp.where(lane == last, behind, inside), 65 + at, 1)
                west[...] = jnp.where((lane >= 64 + at) & (lane < 67 + at), onward, west[...])
        east_ref[0] = east[...].astype(jnp.bfloat16)
        west_ref[0] = west[...].astype(jnp.bfloat16)

    sent = (targets, seats, heights, rows, cols)
    edge = jax.ShapeDtypeStruct((members, channels, pixel_cols), jnp.bfloat16)
    edge_spec = pl.BlockSpec((1, channels, pixel_cols), lambda i: (i, 0, 0))
    return pl.pallas_call(
        kernel,
        grid=(members,),
        out_shape=(
            pltpu.HBM((members, pixel_rows + 2, channels, pixel_cols), jnp.float32),
            edge,
            edge,
            pltpu.HBM(sent, prior_states.dtype),
            jax.ShapeDtypeStruct((members * count,), jnp.int32),
        ),
        in_specs=[
            pl.BlockSpec(memory_space=pltpu.SMEM),
            pl.BlockSpec(memory_space=pltpu.SMEM),
            pl.BlockSpec((1, heights, rows, cols), lambda i: (i, 0, 0, 0)),
            pl.BlockSpec(weights.shape, lambda i: (0, 0, 0, 0)),
            pl.BlockSpec(memory_space=pltpu.HBM),
        ],
        out_specs=(
            pl.BlockSpec((1, pixel_rows + 2, channels, pixel_cols), lambda i: (i, 0, 0, 0)),
            edge_spec,
            edge_spec,
            pl.BlockSpec(memory_space=pltpu.HBM),
            pl.BlockSpec(memory_space=pltpu.SMEM),
        ),
        scratch_shapes=[
            pltpu.VMEM((2, heights * rows, pixel_cols), jnp.float32),
            pltpu.VMEM((2, rows + 8, padded, pixel_cols), jnp.bfloat16),
            pltpu.VMEM((3 * channels, 5 * padded), jnp.bfloat16),
            pltpu.VMEM((2 * channels, 5 * padded), jnp.bfloat16),
            pltpu.VMEM((channels, pixel_cols), jnp.float32),
            pltpu.VMEM((channels, pixel_cols), jnp.float32),
            pltpu.VMEM(sent, prior_states.dtype),
            pltpu.SMEM((targets * count,), jnp.int32),
            pltpu.SMEM((groups,), jnp.int32),
            pltpu.SemaphoreType.DMA((2, targets, seats, count)),
        ],
        compiler_params=pltpu.CompilerParams(
            vmem_limit_bytes=(12 << 20) + 2 * math.prod(sent)
        ),
        name="entry_layer",
    )(ancestors, place, prior_states, weights, prior_states)


def received_sides(from_west, from_east, border):
    west = jnp.where(border[2] == 0, 0.0, from_west.astype(jnp.float32))
    east = jnp.where(border[3] == 0, 0.0, from_east.astype(jnp.float32))
    return west, east


def end_fix(west, east, lane):
    return jnp.where(lax.rem(lane, 3) == 2, west, pltpu.roll(east, 65, 1))


def with_ends(values, fix, row, lane):
    moved = pltpu.roll(fix, (128 - 3 * (row + 2) - 2) % 128, 1)
    return values + jnp.where((lane == 0) | (lane == 127), moved, 0.0)


def side_columns(west, east, own_east, own_west, lane):
    spill = jnp.where(
        lane < 64,
        pltpu.roll(own_west.astype(jnp.float32), 65, 1),
        pltpu.roll(own_east.astype(jnp.float32), 63, 1),
    )
    middle = lax.rem(lax.rem(lane, 64), 3) == 1
    return jnp.where(lane < 64, west, east) + jnp.where(middle, spill, 0.0)


def row_ends(borders, partial, own_east, own_west, from_west, from_east):
    members, row_count, channels, pixel_cols = partial.shape
    tail = row_count // SLOTS - 1

    def kernel(border, top, bottom, own_e, own_w, left, right, north, south):
        lane = lax.broadcasted_iota(jnp.int32, (channels, pixel_cols), 1)
        for member in range(members):
            west, east = received_sides(left[member], right[member], border)
            fix = end_fix(west, east, lane)
            sides = side_columns(west, east, own_e[member], own_w[member], lane)
            for slot in range(SLOTS):
                north[member * SLOTS + slot] = with_ends(top[member, slot], fix, slot - 1, lane).astype(
                    jnp.bfloat16
                )
                south[member * SLOTS + slot] = with_ends(
                    bottom[member, slot], fix, row_count - 4 + slot, lane
                ).astype(jnp.bfloat16)
            line, place = divmod(member, PACKED)
            shown = lax.rem(lane, 64) // 16 == place
            for sent_rows, slot in ((north, 1), (south, row_count - 2)):
                moved = pltpu.roll(sides, (16 * place - 3 * slot) % 128, 1)
                kept = sent_rows[members * SLOTS + line].astype(jnp.float32) if place else 0.0
                sent_rows[members * SLOTS + line] = jnp.where(shown, moved, kept).astype(
                    jnp.bfloat16
                )

    edge_spec = pl.BlockSpec((members, channels, pixel_cols), lambda i: (0, 0, 0))
    rows_spec = (members, SLOTS, channels, pixel_cols)
    sent = (members * SLOTS + pl.cdiv(members, PACKED), channels, pixel_cols)
    return pl.pallas_call(
        kernel,
        grid=(1,),
        out_shape=(jax.ShapeDtypeStruct(sent, jnp.bfloat16),) * 2,
        in_specs=[
            pl.BlockSpec(memory_space=pltpu.SMEM),
            pl.BlockSpec(rows_spec, lambda i: (0, 0, 0, 0)),
            pl.BlockSpec(rows_spec, lambda i: (0, tail, 0, 0)),
            edge_spec,
            edge_spec,
            edge_spec,
            edge_spec,
        ],
        out_specs=(pl.BlockSpec(sent, lambda i: (0, 0, 0)),) * 2,
        compiler_params=pltpu.CompilerParams(vmem_limit_bytes=10 << 20),
        name="row_ends",
    )(
        borders,
        held(partial), held(partial), own_east, own_west, from_west, from_east,
    )


def misfits(borders, partial, sides, rows_in, inner, fixed):
    members, row_count, channels, pixel_cols = partial.shape
    pixel_rows = row_count - 2
    bands = fixed[2].shape[0]
    edge = SLOTS
    whole_rows = rows_in is None
    if whole_rows:
        wanted = list(range(edge, pixel_rows - edge))
        needed = range(edge - 2, pixel_rows - edge + 2)
    else:
        wanted = [*range(edge), *range(pixel_rows - edge, pixel_rows)]
        needed = [*range(-2, edge + 2), *range(pixel_rows - edge - 2, pixel_rows + 2)]

    def kernel(*refs):
        border, pre, own_e, own_w, left, right = refs[:6]
        refs = refs[6:]
        if not whole_rows:
            above, below, above_sides, below_sides, inner_ref = refs[:5]
            refs = refs[5:]
        vectors, weight, matrix_ref, obs, mask_ref = refs[:5]
        out, hidden, taps, side = refs[5:]

        @pl.when(pl.program_id(0) == 0)
        def _():
            for down in range(3):
                line = slice(down * channels, (down + 1) * channels)
                for along in range(3):
                    part = weight[down, along]
                    taps[along * channels : (along + 1) * channels, line] = part
                    if along != 1:
                        half = along // 2 * channels
                        side[half : half + channels, line] = part

        lane = lax.broadcasted_iota(jnp.int32, (channels, pixel_cols), 1)
        bias = jnp.broadcast_to(vectors[:, 0:1], (channels, pixel_cols))
        bias_two = jnp.broadcast_to(vectors[:, 1:2], (channels, pixel_cols))
        offset = jnp.broadcast_to(vectors[:bands, 2:3], (bands, pixel_cols))
        variance = jnp.broadcast_to(vectors[:bands, 3:4], (bands, pixel_cols))
        top, bottom = border[0] == 0, border[1] == 0
        start, end = border[2] == 0, border[3] == 0
        west, east = received_sides(left[0], right[0], border)
        fix = end_fix(west, east, lane)

        for row in needed:
            if row == -2:
                values = above[0].astype(jnp.float32)
            elif row == pixel_rows + 1:
                values = below[SLOTS - 1].astype(jnp.float32)
            else:
                values = with_ends(pre[0, row + 1], fix, row, lane)
                if row <= 0:
                    values = values + above[row + 2].astype(jnp.float32)
                if row >= pixel_rows - 1:
                    values = values + below[row - pixel_rows + 1].astype(jnp.float32)
            values = jnp.maximum(values + bias, 0.0)
            if row < 0:
                values = jnp.where(top, 0.0, values)
            if row >= pixel_rows:
                values = jnp.where(bottom, 0.0, values)
            hidden[row + 2] = values.astype(jnp.bfloat16)

        slot = lax.div(lax.rem(lane, 64), 3)
        cells = side_columns(west, east, own_e[0], own_w[0], lane)
        outside = (start & (lane < 64)) | (end & (lane >= 64))
        if not whole_rows:
            place = 16 * lax.rem(pl.program_id(0), PACKED)
            upper = pltpu.roll(
                above_sides[0].astype(jnp.float32), lax.rem(pixel_cols - place, pixel_cols), 1
            )
            lower = pltpu.roll(
                below_sides[0].astype(jnp.float32), 3 * (pixel_rows + 1) - place + (
                    0 if 3 * (pixel_rows + 1) >= 16 * (PACKED - 1) else pixel_cols
                ), 1
            )
            cells = (
                cells
                + jnp.where(slot < 3, upper, 0.0)
                + jnp.where((slot > pixel_rows) & (slot < pixel_rows + 4), lower, 0.0)
            )
            outside = outside | (top & (slot < 2)) | (bottom & (slot >= pixel_rows + 2))
        cells = jnp.where(outside, 0.0, jnp.maximum(cells + bias, 0.0))
        stack = jnp.concatenate(
            [pltpu.roll(cells, 6, 1), cells, pltpu.roll(cells, 122, 1)], axis=0
        ).astype(jnp.bfloat16)
        found = jnp.dot(side[...], stack, preferred_element_type=jnp.float32)
        column = jnp.where(lane < 64, found[:channels], found[channels:])

        def window(row):
            return jnp.concatenate([hidden[row], hidden[row + 2], hidden[row + 4]], axis=0)

        if not whole_rows:
            out[0, edge : pixel_rows - edge] = inner_ref[0, edge : pixel_rows - edge]
        for first, second in zip(wanted[::2], wanted[1::2]):
            both = jnp.dot(
                taps[...],
                jnp.concatenate([window(first), window(second)], axis=1),
                preferred_element_type=jnp.float32,
            )
            ready = []
            for half, row in enumerate((first, second)):
                parts = both[:, half * pixel_cols : (half + 1) * pixel_cols]
                at = 3 * (row + 2)
                values = (
                    parts[channels : 2 * channels]
                    + jnp.where(
                        lane < 2,
                        pltpu.roll(column, 128 - at, 1),
                        pltpu.roll(parts[:channels], 2, 1),
                    )
                    + jnp.where(
                        lane >= 126,
                        pltpu.roll(column, (189 - at) % 128, 1),
                        pltpu.roll(parts[2 * channels :], 126, 1),
                    )
                )
                ready.append(jnp.maximum(values + bias_two, 0.0).astype(jnp.bfloat16))
            predicted = jnp.dot(
                matrix_ref[...],
                jnp.concatenate(ready, axis=1),
                preferred_element_type=jnp.float32,
            )
            for half, row in enumerate((first, second)):
                misfit = obs[pl.ds(row, bands, stride=pixel_rows), :] - (
                    predicted[:, half * pixel_cols : (half + 1) * pixel_cols] + offset
                )
                total = jnp.sum(misfit * misfit / variance, axis=0, keepdims=True)
                out[0, row : row + 1] = total * mask_ref[row : row + 1].astype(jnp.float32)

    edge_spec = pl.BlockSpec((1, channels, pixel_cols), lambda i: (i, 0, 0))
    line_spec = pl.BlockSpec((SLOTS, channels, pixel_cols), lambda i: (i, 0, 0))
    packed_spec = pl.BlockSpec(
        (1, channels, pixel_cols), lambda i: (members * SLOTS + lax.div(i, PACKED), 0, 0)
    )
    out_spec = pl.BlockSpec((1, pixel_rows, pixel_cols), lambda i: (i, 0, 0))

    def whole(array):
        return pl.BlockSpec(array.shape, lambda i, n=array.ndim: (0,) * n)

    extra = () if whole_rows else (*rows_in, *rows_in, inner)
    extra_specs = [] if whole_rows else [line_spec] * 2 + [packed_spec] * 2 + [out_spec]
    return pl.pallas_call(
        kernel,
        grid=(members,),
        out_shape=jax.ShapeDtypeStruct((members, pixel_rows, pixel_cols), jnp.float32),
        in_specs=[
            pl.BlockSpec(memory_space=pltpu.SMEM),
            pl.BlockSpec((1, row_count, channels, pixel_cols), lambda i: (i, 0, 0, 0)),
        ]
        + [edge_spec] * 4
        + extra_specs
        + [whole(array) for array in fixed],
        out_specs=out_spec,
        scratch_shapes=[
            pltpu.VMEM((pixel_rows + 4, channels, pixel_cols), jnp.bfloat16),
            pltpu.VMEM((3 * channels, 3 * channels), jnp.bfloat16),
            pltpu.VMEM((2 * channels, 3 * channels), jnp.bfloat16),
        ],
        compiler_params=pltpu.CompilerParams(vmem_limit_bytes=8 << 20),
        name="inner_misfits" if whole_rows else "outer_misfits",
    )(borders, held(partial), *sides, *extra, *[held(x) for x in fixed])


def neighbours(axis):
    count = lax.axis_size(axis)
    onward = [(i, i + 1) for i in range(count - 1)]
    return onward, [(j, i) for i, j in onward]


def departures(
    ancestors,
    place,
    targets,
    seats,
    prior_states,
    measured_brightness,
    measured_indicator,
    sensor_error_spread,
    entry_layer_stencil,
    entry_layer_offset,
    middle_layer_stencil,
    middle_layer_offset,
    brightness_matrix,
    brightness_offset,
):
    channels = entry_layer_stencil.shape[0]
    lat, lon = lax.axis_index("lat"), lax.axis_index("lon")
    borders = jnp.stack(
        [lat, lax.axis_size("lat") - 1 - lat, lon, lax.axis_size("lon") - 1 - lon]
    ).astype(jnp.int32)
    partial, own_east, own_west, picked, table = entry_layer(
        ancestors,
        place,
        held(prior_states),
        held(jnp.transpose(entry_layer_stencil, (2, 3, 1, 0))),
        targets,
        seats,
    )
    count = lax.axis_size("lon")
    ring = [(i, (i + 1) % count) for i in range(count)]
    from_west = lax.ppermute(own_east, "lon", ring)
    from_east = lax.ppermute(own_west, "lon", [(j, i) for i, j in ring])
    sides = (own_east, own_west, from_west, from_east)
    north, south = row_ends(borders, partial, *sides)
    onward, back = neighbours("lat")
    from_north = lax.ppermute(south, "lat", onward)
    from_south = lax.ppermute(north, "lat", back)
    bands = brightness_matrix.shape[0]
    vectors = jnp.stack(
        [
            entry_layer_offset,
            middle_layer_offset,
            jnp.pad(brightness_offset, (0, channels - bands)),
            jnp.pad(sensor_error_spread, (0, channels - bands), constant_values=1.0),
        ],
        axis=1,
    )
    fixed = (
        vectors,
        jnp.transpose(middle_layer_stencil, (2, 3, 0, 1)),
        brightness_matrix,
        measured_brightness.reshape(-1, measured_brightness.shape[-1]),
        measured_indicator,
    )
    inner = misfits(borders, partial, sides, None, None, fixed)
    squares = misfits(borders, partial, sides, (from_north, from_south), inner, fixed)
    return squares, picked, table, borders


def chunk_of(heights):
    return next(size for size in (5, 4, 2, 1) if heights % size == 0)


def body(prior_states, *rest):
    ancestor_indices = rest[-1]
    members, heights, rows, cols = prior_states.shape
    groups = lax.axis_size("ens")
    own = lax.axis_index("ens").astype(jnp.int32)
    seats = max(2, (members + groups - 1) // groups)
    ancestors = jnp.transpose(ancestor_indices, (1, 2, 0)).reshape(-1, ancestor_indices.shape[0])
    swap = [(0, 1), (1, 0)]
    paired = groups == 2
    if paired:
        targets = (1 - own)[None]
    else:
        targets = jnp.arange(groups, dtype=jnp.int32)
    place = jnp.concatenate([own[None], targets])
    squares, picked, table, borders = departures(
        ancestors, place, targets.shape[0], seats, prior_states, *rest[:-1]
    )
    if paired:
        received = lax.ppermute(picked, "ens", swap)
    else:
        received = lax.all_to_all(picked, "ens", split_axis=0, concat_axis=0, tiled=True)
    band_lat = taper_band(squares.shape[1], RADIUS)
    padded = extended(squares, (("lat", 1),), RADIUS)
    smooth = jnp.einsum("ij,pjk->pik", band_lat, padded, precision=lax.Precision.HIGHEST)
    pixel_cols = squares.shape[2]
    band_lon = np.zeros((3 * pixel_cols, pixel_cols), np.float32)
    near = slice(pixel_cols - RADIUS, 2 * pixel_cols + RADIUS)
    band_lon[near] = taper_band(pixel_cols, RADIUS).T
    count = lax.axis_size("lon")
    ring = [(i, (i + 1) % count) for i in range(count)]
    from_west = lax.ppermute(smooth, "lon", ring)
    from_east = lax.ppermute(smooth, "lon", [(j, i) for i, j in ring])
    size = chunk_of(heights)
    pieces = PIECES if heights // size % PIECES == 0 else 1
    levels = heights // pieces
    field = prior_states
    scaled, own_norm, own_mean, *sent = group_mean(
        borders, smooth, from_west, from_east, band_lon, field, pieces, size
    )
    if paired:
        other_norm = lax.ppermute(own_norm, "ens", swap)
        others = [lax.ppermute(piece, "ens", swap) for piece in sent]
    else:
        peak = lax.pmax(own_norm[0], "ens")
        part = own_norm[1] * jnp.exp(own_norm[0] - peak)
        total, added = lax.psum((part, expand_patches(part)[None] * own_mean), "ens")
        own_mean = added / expand_patches(total)[None]
        other_norm = jnp.stack([peak, total])
        others = sent
    weights, parts = merge(scaled, own_norm, other_norm, not paired)
    analysis = None
    for k, other_mean in enumerate(others):
        analysis = combine(
            table, parts, own_mean, other_mean, field, received, analysis, k * levels, size
        )
    return analysis, weights


def solution(mesh):
    return jax.shard_map(
        body,
        mesh=mesh,
        in_specs=(
            P("ens", None, "lat", "lon"),
            P(None, "lat", "lon"),
            P("lat", "lon"),
            P(),
            P(),
            P(),
            P(),
            P(),
            P(),
            P(),
            P(None, "lat", "lon"),
        ),
        out_specs=(P("ens", None, "lat", "lon"), P("ens", "lat", "lon")),
        check_vma=False,
    )
```

```python
import math

import jax
import jax.numpy as jnp
from jax import lax
from jax.experimental import pallas as pl
from jax.experimental.pallas import tpu as pltpu
from jax.sharding import PartitionSpec as P
import numpy as np

PATCH_NORTHWARD = 32
PATCH_EASTWARD = 128
RADIUS = 16


relax_factor = 0.6
PIECES = 4


def extended(shard, sides, width):
    for axis, dim in sides:
        peers, length = (lax.axis_size(axis), shard.shape[dim])
        up = [(i, (i + 1) % peers) for i in range(peers - 1)]
        down = [(j, i) for i, j in up]
        last = lax.slice_in_dim(shard, length - width, length, axis=dim)
        first = lax.slice_in_dim(shard, 0, width, axis=dim)
        before = lax.ppermute(last, axis, up)
        after = lax.ppermute(first, axis, down)
        shard = jnp.concatenate([before, shard, after], axis=dim)
    return shard


def taper_band(inner_count, radius):
    tap_count = 2 * radius + 1
    tap_width = radius / 2.0
    taps = np.exp(-0.5 * ((np.arange(tap_count) - radius) / tap_width) ** 2)
    taps = taps / taps.sum()
    band = np.zeros((inner_count, inner_count + 2 * radius), np.float32)
    for out_index in range(inner_count):
        band[out_index, out_index : out_index + tap_count] = taps
    return band


def expand_patches(values):
    lead = values.shape[:-2]
    rows, cols = (values.shape[-2], values.shape[-1])
    grown = jnp.broadcast_to(values[..., :, None, :, None], lead + (rows, 2, cols, 2))
    return grown.reshape(lead + (rows * 2, cols * 2))


LANES = 128


def held(array):
    return pltpu.with_memory_space_constraint(array, pltpu.HBM)


def store_doubled(out, values):
    count, rows, cols = values.shape
    of_cols = lax.broadcasted_iota(jnp.int32, (cols, 2 * cols), 0)
    to_cols = lax.broadcasted_iota(jnp.int32, (cols, 2 * cols), 1)
    wide = (lax.shift_right_logical(to_cols, 1) == of_cols).astype(jnp.float32)
    wide = wide.astype(jnp.bfloat16)
    rest = values.reshape(count * rows, cols)
    grown = None
    for _ in range(3):
        part = rest.astype(jnp.bfloat16)
        rest = rest - part.astype(jnp.float32)
        moved = jnp.dot(part, wide, preferred_element_type=jnp.float32)
        grown = moved if grown is None else grown + moved
    for which in range(count):
        for block in range(2 * cols // LANES):
            piece = grown[which * rows : (which + 1) * rows, block * LANES : (block + 1) * LANES]
            for half in range(2):
                out[which, block, pl.ds(half, rows, stride=2), :] = piece


def tiles_of(rows, cols):
    return [
        (north, east)
        for north in range(rows // PATCH_NORTHWARD)
        for east in range(cols // PATCH_EASTWARD)
    ]


def tile_window(north, east):
    return (
        pl.ds(north * PATCH_NORTHWARD, PATCH_NORTHWARD),
        pl.ds(east * PATCH_EASTWARD, PATCH_EASTWARD),
    )


def group_mean(borders, smooth, from_west, from_east, band, prior_states, pieces, chunk):
    members, pixel_rows, pixel_cols = smooth.shape
    _, heights, rows, cols = prior_states.shape
    blocks = cols // LANES
    per_piece = heights // chunk // pieces

    def kernel(border, own_ref, left, right, band_ref, prior, scaled_ref, norm_ref, mean_ref, *refs):
        sent, share = refs[:pieces], refs[pieces]
        step = pl.program_id(0)

        @pl.when(step == 0)
        def _():
            west = jnp.where(border[2] == 0, 0.0, left[...])
            east = jnp.where(border[3] == 0, 0.0, right[...])
            padded = jnp.concatenate([west, own_ref[...], east], axis=2)
            tapered = jnp.dot(
                padded.reshape(members * pixel_rows, 3 * pixel_cols),
                band_ref[...],
                precision=lax.Precision.HIGHEST,
            )
            values = -0.5 * tapered.reshape(members, pixel_rows, pixel_cols)
            peak = jnp.max(values, axis=0)
            scaled = jnp.exp(values - peak[None])
            total = jnp.sum(scaled, axis=0)
            scaled_ref[...] = scaled
            norm_ref[0] = peak
            norm_ref[1] = total
            store_doubled(share, scaled / total[None])

        for block in range(blocks):
            window = slice(block * LANES, (block + 1) * LANES)
            for level in range(chunk):
                mean = share[0, block] * prior[0, level, :, window].astype(jnp.float32)
                for member in range(1, members):
                    mean = mean + share[member, block] * prior[member, level, :, window].astype(
                        jnp.float32
                    )
                mean_ref[level, :, window] = mean
        for piece in range(pieces):

            @pl.when((step >= piece * per_piece) & (step < (piece + 1) * per_piece))
            def _(piece=piece):
                sent[piece][...] = mean_ref[...].astype(jnp.bfloat16)

    def whole(shape):
        return pl.BlockSpec(shape, lambda i, n=len(shape): (0,) * n)

    def piece_spec(piece):
        return pl.BlockSpec(
            (chunk, rows, cols),
            lambda i: (jnp.clip(i - piece * per_piece, 0, per_piece - 1), 0, 0),
        )

    norm = (2, pixel_rows, pixel_cols)
    return pl.pallas_call(
        kernel,
        grid=(heights // chunk,),
        out_shape=(
            pltpu.HBM(smooth.shape, jnp.float32),
            pltpu.HBM(norm, jnp.float32),
            jax.ShapeDtypeStruct((heights, rows, cols), jnp.float32),
        )
        + (jax.ShapeDtypeStruct((heights // pieces, rows, cols), jnp.bfloat16),) * pieces,
        in_specs=[
            pl.BlockSpec(memory_space=pltpu.SMEM),
            whole(smooth.shape),
            whole(smooth.shape),
            whole(smooth.shape),
            whole(band.shape),
            pl.BlockSpec((members, chunk, rows, cols), lambda i: (0, i, 0, 0)),
        ],
        out_specs=(
            whole(smooth.shape),
            whole(norm),
            pl.BlockSpec((chunk, rows, cols), lambda i: (i, 0, 0)),
        )
        + tuple(piece_spec(piece) for piece in range(pieces)),
        scratch_shapes=[pltpu.VMEM((members, blocks, rows, LANES), jnp.float32)],
        compiler_params=pltpu.CompilerParams(vmem_limit_bytes=16 << 20),
        name="group_mean",
    )(borders, smooth, from_west, from_east, band, prior_states)


def merge(scaled, own_norm, other_norm, shared):
    _, pixel_rows, pixel_cols = scaled.shape

    def kernel(scaled_ref, own_ref, other_ref, weights, parts):
        own_peak, own_total = own_ref[0], own_ref[1]
        other_peak, other_total = other_ref[0], other_ref[1]
        peak = jnp.maximum(own_peak, other_peak)
        own_scale = jnp.exp(own_peak - peak)
        own_part = own_total * own_scale
        if shared:
            total = other_total
            weighted = jnp.stack([jnp.ones_like(total), jnp.zeros_like(total)])
        else:
            other_part = other_total * jnp.exp(other_peak - peak)
            total = own_part + other_part
            weighted = jnp.stack([own_part, other_part]) / total[None]
        store_doubled(parts, (1.0 - relax_factor) * weighted)
        weights[...] = scaled_ref[...] * (own_scale / total)[None]

    return pl.pallas_call(
        kernel,
        out_shape=(
            jax.ShapeDtypeStruct(scaled.shape, jnp.float32),
            pltpu.HBM((2, 2 * pixel_cols // LANES, 2 * pixel_rows, LANES), jnp.float32),
        ),
        name="merge",
    )(held(scaled), held(own_norm), other_norm)


def combine(table, parts, own_mean, other_mean, prior_states, received, analysis, first, chunk):
    members, heights, rows, cols = prior_states.shape
    tiles = tiles_of(rows, cols)
    count = len(tiles)
    sources, seats = received.shape[:2]
    received = received.reshape((sources * seats,) + received.shape[2:])
    steps = other_mean.shape[0] // chunk
    start = first // chunk
    done = () if analysis is None else (analysis,)

    def kernel(lookup, parts_ref, mean_ref, peer_ref, prior, remote, *refs):
        analysis_ref, out, base, sems = refs[len(done) :]
        step = pl.program_id(0)
        half = lax.rem(step, 2)

        def leave(at, slot, which):
            return pltpu.make_async_copy(
                out.at[which, slot],
                analysis_ref.at[slot, pl.ds(first + at * chunk, chunk)],
                sems.at[which, slot],
            )

        for block in range(cols // LANES):
            window = slice(block * LANES, (block + 1) * LANES)
            for level in range(chunk):
                base[level, :, window] = parts_ref[0, block] * mean_ref[
                    level, :, window
                ] + parts_ref[1, block] * peer_ref[level, :, window].astype(jnp.float32)

        def fill(array, source, slot, tile):
            north, east = tiles[tile]
            down = slice(north * PATCH_NORTHWARD, (north + 1) * PATCH_NORTHWARD)
            along = slice(east * PATCH_EASTWARD, (east + 1) * PATCH_EASTWARD)
            for level in range(chunk):
                out[half, slot, level, down, along] = base[level, down, along] + relax_factor * array[
                    source, level, down, along
                ].astype(jnp.float32)

        for slot in range(members):

            @pl.when(step >= 2)
            def _(slot=slot):
                leave(step - 2, slot, half).wait()

            for tile in range(count):
                source = lookup[slot * count + tile]

                @pl.when(source < members)
                def _(slot=slot, tile=tile, source=source):
                    fill(prior, source, slot, tile)

                @pl.when(source >= members)
                def _(slot=slot, tile=tile, source=source):
                    fill(remote, source - members, slot, tile)

            leave(step, slot, half).start()

        @pl.when(step == steps - 1)
        def _():
            for slot in range(members):
                if steps > 1:
                    leave(step - 1, slot, 1 - half).wait()
                leave(step, slot, half).wait()

    return pl.pallas_call(
        kernel,
        grid=(steps,),
        out_shape=jax.ShapeDtypeStruct(prior_states.shape, jnp.float32),
        in_specs=[
            pl.BlockSpec(memory_space=pltpu.SMEM),
            pl.BlockSpec(parts.shape, lambda i: (0, 0, 0, 0)),
            pl.BlockSpec((chunk, rows, cols), lambda i: (start + i, 0, 0)),
            pl.BlockSpec((chunk, rows, cols), lambda i: (i, 0, 0)),
            pl.BlockSpec((members, chunk, rows, cols), lambda i: (0, start + i, 0, 0)),
            pl.BlockSpec((sources * seats, chunk, rows, cols), lambda i: (0, start + i, 0, 0)),
        ]
        + [pl.BlockSpec(memory_space=pltpu.HBM)] * len(done),
        out_specs=pl.BlockSpec(memory_space=pltpu.HBM),
        input_output_aliases={6: 0} if done else {},
        scratch_shapes=[
            pltpu.VMEM((2, members, chunk, rows, cols), jnp.float32),
            pltpu.VMEM((chunk, rows, cols), jnp.float32),
            pltpu.SemaphoreType.DMA((2, members)),
        ],
        compiler_params=pltpu.CompilerParams(vmem_limit_bytes=12 << 20),
        name="combine",
    )(table, held(parts), own_mean, other_mean, held(prior_states), held(received), *done)


SLOTS = 3
PACKED = 4


def entry_layer(ancestors, place, prior_states, weights, targets, seats, span, earlier):
    begin, steps = span[0], span[1] - span[0]
    picking = earlier is None
    members, heights, rows, cols = prior_states.shape
    tiles = tiles_of(rows, cols)
    count = len(tiles)
    groups = ancestors.shape[1] // members
    channels = weights.shape[-1]
    padded = pl.cdiv(heights, 16) * 16
    pixel_rows, pixel_cols = rows // 2, cols // 2

    def kernel(
        ancestor, spot, prior, *refs
    ):
        if picking:
            weight, field, out, east_ref, west_ref, picked, table, even_ref, odd_ref = refs[:9]
            sorted_cells, lines, east, west, buffer, used, seen, sems = refs[9:]
        else:
            even_ref, odd_ref = refs[:2]
            out, east_ref, west_ref, sorted_cells, lines, east, west = refs[5:]

        def transfer(target, seat, member, tile, leaving):
            window = tile_window(*tiles[tile])
            here = buffer.at[(target, seat, slice(None)) + window]
            sem = sems.at[int(leaving), target, seat, tile]
            if leaving:
                away = picked.at[(target, seat, slice(None)) + window]
                return pltpu.make_async_copy(here, away, sem)
            return pltpu.make_async_copy(field.at[(member, slice(None)) + window], here, sem)

        def each_seat(action):
            for target in range(targets):
                for tile in range(count):
                    for seat in range(seats):

                        @pl.when(seat < used[target * count + tile])
                        def _(target=target, tile=tile, seat=seat):
                            action(target, seat, tile)

        def load_then_send(target, seat, tile):
            transfer(target, seat, 0, tile, False).wait()
            transfer(target, seat, 0, tile, True).start()

        def note_parents():
            own = spot[0]
            for target in range(targets):
                for tile in range(count):
                    rank = jnp.int32(0)
                    for slot in range(members):
                        parent = ancestor[tile, spot[1 + target] * members + slot]
                        local = parent - own * members
                        hit = (local >= 0) & (local < members) & (rank < seats)

                        @pl.when(hit)
                        def _(target=target, rank=rank, local=local, tile=tile):
                            transfer(target, rank, local, tile, False).start()

                        rank = rank + hit.astype(jnp.int32)
                    used[target * count + tile] = rank
            for tile in range(count):
                for group in range(groups):
                    seen[group] = 0
                for slot in range(members):
                    parent = ancestor[tile, own * members + slot]
                    group = lax.div(parent, jnp.int32(members))
                    rank = seen[group]
                    seen[group] = rank + 1
                    line = (jnp.int32(0) if targets == 1 else group) * seats + rank
                    table[slot * count + tile] = jnp.where(
                        group == own, parent - own * members, members + line
                    )
        @pl.when(pl.program_id(0) == 0)
        def _():
            if picking:
                note_parents()
                even_ref[...] = jnp.zeros_like(even_ref)
                odd_ref[...] = jnp.zeros_like(odd_ref)
                for down in range(5):
                    for along in range(5):
                        part = weight[down, along].astype(jnp.float32).T.astype(jnp.bfloat16)
                        taps = odd_ref if along % 2 else even_ref
                        line = along // 2 * channels
                        taps[line : line + channels, down * padded : down * padded + heights] = part
            lines[...] = jnp.zeros_like(lines)

        if picking:

            @pl.when(pl.program_id(0) == steps // 2)
            def _():
                each_seat(load_then_send)

        here = lax.broadcasted_iota(jnp.int32, (cols, cols), 0)
        there = lax.broadcasted_iota(jnp.int32, (cols, cols), 1)
        chosen = jnp.where(there < pixel_cols, 2 * there, 2 * (there - pixel_cols) + 1)
        parity = (here == chosen).astype(jnp.float32).astype(jnp.bfloat16)
        split = jnp.dot(
            prior[0].reshape(heights * rows, cols), parity, preferred_element_type=jnp.float32
        )
        for kind in range(2):
            sorted_cells[kind] = split[:, kind * pixel_cols : (kind + 1) * pixel_cols]
        for kind in range(2):
            for row in range(rows):
                lines[kind, row + 4, :heights] = sorted_cells[
                    kind, pl.ds(row, heights, stride=rows), :
                ].astype(jnp.bfloat16)
        east[...] = jnp.zeros_like(east)
        west[...] = jnp.zeros_like(west)
        lane = lax.broadcasted_iota(jnp.int32, (channels, pixel_cols), 1)
        last = pixel_cols - 1

        def window(kind, row):
            return lines[kind, 2 * row + 2 : 2 * row + 7].reshape(5 * padded, pixel_cols)

        for pair in range(-1, pixel_rows + 1, 2):
            even, odd = (
                jnp.dot(
                    taps[...],
                    jnp.concatenate([window(kind, pair), window(kind, pair + 1)], axis=1),
                    preferred_element_type=jnp.float32,
                )
                for kind, taps in ((0, even_ref), (1, odd_ref))
            )
            for half in range(2):
                row = pair + half
                here_even = even[:, half * pixel_cols : (half + 1) * pixel_cols]
                here_odd = odd[:, half * pixel_cols : (half + 1) * pixel_cols]
                ahead = pltpu.roll(here_even[:channels] + here_odd[:channels], 1, 1)
                behind = pltpu.roll(here_even[2 * channels :], last, 1)
                inside = (
                    here_even[channels : 2 * channels]
                    + here_odd[channels:]
                    + jnp.where(lane == 0, 0.0, ahead)
                    + jnp.where(lane == last, 0.0, behind)
                )
                out[0, row + 1] = inside
                at = 3 * (row + 2)
                onward = pltpu.roll(jnp.where(lane == 0, ahead, inside), at + 2, 1)
                east[...] = jnp.where((lane >= at) & (lane < at + 3), onward, east[...])
                onward = pltpu.roll(jnp.where(lane == last, behind, inside), 65 + at, 1)
                west[...] = jnp.where((lane >= 64 + at) & (lane < 67 + at), onward, west[...])
        east_ref[0] = east[...].astype(jnp.bfloat16)
        west_ref[0] = west[...].astype(jnp.bfloat16)
        if picking:

            @pl.when(pl.program_id(0) == steps - 1)
            def _():
                each_seat(lambda target, seat, tile: transfer(target, seat, 0, tile, True).wait())

    sent = (targets, seats, heights, rows, cols)
    picked_shapes = (
        pltpu.HBM(sent, prior_states.dtype),
        jax.ShapeDtypeStruct((members * count,), jnp.int32),
        jax.ShapeDtypeStruct((3 * channels, 5 * padded), prior_states.dtype),
        jax.ShapeDtypeStruct((2 * channels, 5 * padded), prior_states.dtype),
    )
    tap_specs = [
        pl.BlockSpec((size * channels, 5 * padded), lambda i: (0, 0)) for size in (3, 2)
    ]
    edge = jax.ShapeDtypeStruct((members, channels, pixel_cols), jnp.bfloat16)
    edge_spec = pl.BlockSpec((1, channels, pixel_cols), lambda i: (begin + i, 0, 0))
    return pl.pallas_call(
        kernel,
        grid=(steps,),
        out_shape=(
            pltpu.HBM((members, pixel_rows + 2, channels, pixel_cols), jnp.float32),
            edge,
            edge,
        )
        + picked_shapes * picking,
        in_specs=[
            pl.BlockSpec(memory_space=pltpu.SMEM),
            pl.BlockSpec(memory_space=pltpu.SMEM),
            pl.BlockSpec((1, heights, rows, cols), lambda i: (begin + i, 0, 0, 0)),
        ]
        + (
            [
                pl.BlockSpec(weights.shape, lambda i: (0, 0, 0, 0)),
                pl.BlockSpec(memory_space=pltpu.HBM),
            ]
            if picking
            else tap_specs + [pl.BlockSpec(memory_space=pltpu.HBM)] * 3
        ),
        out_specs=(
            pl.BlockSpec((1, pixel_rows + 2, channels, pixel_cols), lambda i: (begin + i, 0, 0, 0)),
            edge_spec,
            edge_spec,
        )
        + (pl.BlockSpec(memory_space=pltpu.HBM), pl.BlockSpec(memory_space=pltpu.SMEM), *tap_specs)
        * picking,
        input_output_aliases={} if picking else {5: 0, 6: 1, 7: 2},
        scratch_shapes=[
            pltpu.VMEM((2, heights * rows, pixel_cols), jnp.float32),
            pltpu.VMEM((2, rows + 8, padded, pixel_cols), jnp.bfloat16),
            pltpu.VMEM((channels, pixel_cols), jnp.float32),
            pltpu.VMEM((channels, pixel_cols), jnp.float32),
        ]
        + [
            pltpu.VMEM(sent, prior_states.dtype),
            pltpu.SMEM((targets * count,), jnp.int32),
            pltpu.SMEM((groups,), jnp.int32),
            pltpu.SemaphoreType.DMA((2, targets, seats, count)),
        ]
        * picking,
        compiler_params=pltpu.CompilerParams(
            vmem_limit_bytes=(12 << 20) + 2 * math.prod(sent)
        ),
        name="entry_layer",
    )(ancestors, place, prior_states, *(earlier or (weights, prior_states)))


def received_sides(from_west, from_east, border):
    west = jnp.where(border[2] == 0, 0.0, from_west.astype(jnp.float32))
    east = jnp.where(border[3] == 0, 0.0, from_east.astype(jnp.float32))
    return west, east


def end_fix(west, east, lane):
    return jnp.where(lax.rem(lane, 3) == 2, west, pltpu.roll(east, 65, 1))


def with_ends(values, fix, row, lane):
    moved = pltpu.roll(fix, (128 - 3 * (row + 2) - 2) % 128, 1)
    return values + jnp.where((lane == 0) | (lane == 127), moved, 0.0)


def side_columns(west, east, own_east, own_west, lane):
    spill = jnp.where(
        lane < 64,
        pltpu.roll(own_west.astype(jnp.float32), 65, 1),
        pltpu.roll(own_east.astype(jnp.float32), 63, 1),
    )
    middle = lax.rem(lax.rem(lane, 64), 3) == 1
    return jnp.where(lane < 64, west, east) + jnp.where(middle, spill, 0.0)


def row_ends(borders, partial, own_east, own_west, from_west, from_east):
    members, row_count, channels, pixel_cols = partial.shape
    tail = row_count // SLOTS - 1

    def kernel(border, top, bottom, own_e, own_w, left, right, north, south):
        lane = lax.broadcasted_iota(jnp.int32, (channels, pixel_cols), 1)
        for member in range(members):
            west, east = received_sides(left[member], right[member], border)
            fix = end_fix(west, east, lane)
            sides = side_columns(west, east, own_e[member], own_w[member], lane)
            for slot in range(SLOTS):
                north[member * SLOTS + slot] = with_ends(top[member, slot], fix, slot - 1, lane).astype(
                    jnp.bfloat16
                )
                south[member * SLOTS + slot] = with_ends(
                    bottom[member, slot], fix, row_count - 4 + slot, lane
                ).astype(jnp.bfloat16)
            line, place = divmod(member, PACKED)
            shown = lax.rem(lane, 64) // 16 == place
            for sent_rows, slot in ((north, 1), (south, row_count - 2)):
                moved = pltpu.roll(sides, (16 * place - 3 * slot) % 128, 1)
                kept = sent_rows[members * SLOTS + line].astype(jnp.float32) if place else 0.0
                sent_rows[members * SLOTS + line] = jnp.where(shown, moved, kept).astype(
                    jnp.bfloat16
                )

    edge_spec = pl.BlockSpec((members, channels, pixel_cols), lambda i: (0, 0, 0))
    rows_spec = (members, SLOTS, channels, pixel_cols)
    sent = (members * SLOTS + pl.cdiv(members, PACKED), channels, pixel_cols)
    return pl.pallas_call(
        kernel,
        grid=(1,),
        out_shape=(jax.ShapeDtypeStruct(sent, jnp.bfloat16),) * 2,
        in_specs=[
            pl.BlockSpec(memory_space=pltpu.SMEM),
            pl.BlockSpec(rows_spec, lambda i: (0, 0, 0, 0)),
            pl.BlockSpec(rows_spec, lambda i: (0, tail, 0, 0)),
            edge_spec,
            edge_spec,
            edge_spec,
            edge_spec,
        ],
        out_specs=(pl.BlockSpec(sent, lambda i: (0, 0, 0)),) * 2,
        compiler_params=pltpu.CompilerParams(vmem_limit_bytes=10 << 20),
        name="row_ends",
    )(
        borders,
        held(partial), held(partial), own_east, own_west, from_west, from_east,
    )


def misfits(borders, partial, sides, rows_in, inner, fixed):
    members, row_count, channels, pixel_cols = partial.shape
    pixel_rows = row_count - 2
    bands = fixed[2].shape[0]
    edge = SLOTS
    whole_rows = rows_in is None
    if whole_rows:
        wanted = list(range(edge, pixel_rows - edge))
        needed = range(edge - 2, pixel_rows - edge + 2)
    else:
        wanted = [*range(edge), *range(pixel_rows - edge, pixel_rows)]
        needed = [*range(-2, edge + 2), *range(pixel_rows - edge - 2, pixel_rows + 2)]

    def kernel(*refs):
        border, pre, own_e, own_w, left, right = refs[:6]
        refs = refs[6:]
        if not whole_rows:
            above, below, above_sides, below_sides, inner_ref = refs[:5]
            refs = refs[5:]
        vectors, weight, matrix_ref, obs, mask_ref = refs[:5]
        out, hidden, taps, side = refs[5:]

        @pl.when(pl.program_id(0) == 0)
        def _():
            for down in range(3):
                line = slice(down * channels, (down + 1) * channels)
                for along in range(3):
                    part = weight[down, along]
                    taps[along * channels : (along + 1) * channels, line] = part
                    if along != 1:
                        half = along // 2 * channels
                        side[half : half + channels, line] = part

        lane = lax.broadcasted_iota(jnp.int32, (channels, pixel_cols), 1)
        bias = jnp.broadcast_to(vectors[:, 0:1], (channels, pixel_cols))
        bias_two = jnp.broadcast_to(vectors[:, 1:2], (channels, pixel_cols))
        offset = jnp.broadcast_to(vectors[:bands, 2:3], (bands, pixel_cols))
        variance = jnp.broadcast_to(vectors[:bands, 3:4], (bands, pixel_cols))
        top, bottom = border[0] == 0, border[1] == 0
        start, end = border[2] == 0, border[3] == 0
        west, east = received_sides(left[0], right[0], border)
        fix = end_fix(west, east, lane)

        for row in needed:
            if row == -2:
                values = above[0].astype(jnp.float32)
            elif row == pixel_rows + 1:
                values = below[SLOTS - 1].astype(jnp.float32)
            else:
                values = with_ends(pre[0, row + 1], fix, row, lane)
                if row <= 0:
                    values = values + above[row + 2].astype(jnp.float32)
                if row >= pixel_rows - 1:
                    values = values + below[row - pixel_rows + 1].astype(jnp.float32)
            values = jnp.maximum(values + bias, 0.0)
            if row < 0:
                values = jnp.where(top, 0.0, values)
            if row >= pixel_rows:
                values = jnp.where(bottom, 0.0, values)
            hidden[row + 2] = values.astype(jnp.bfloat16)

        slot = lax.div(lax.rem(lane, 64), 3)
        cells = side_columns(west, east, own_e[0], own_w[0], lane)
        outside = (start & (lane < 64)) | (end & (lane >= 64))
        if not whole_rows:
            place = 16 * lax.rem(pl.program_id(0), PACKED)
            upper = pltpu.roll(
                above_sides[0].astype(jnp.float32), lax.rem(pixel_cols - place, pixel_cols), 1
            )
            lower = pltpu.roll(
                below_sides[0].astype(jnp.float32), 3 * (pixel_rows + 1) - place + (
                    0 if 3 * (pixel_rows + 1) >= 16 * (PACKED - 1) else pixel_cols
                ), 1
            )
            cells = (
                cells
                + jnp.where(slot < 3, upper, 0.0)
                + jnp.where((slot > pixel_rows) & (slot < pixel_rows + 4), lower, 0.0)
            )
            outside = outside | (top & (slot < 2)) | (bottom & (slot >= pixel_rows + 2))
        cells = jnp.where(outside, 0.0, jnp.maximum(cells + bias, 0.0))
        stack = jnp.concatenate(
            [pltpu.roll(cells, 6, 1), cells, pltpu.roll(cells, 122, 1)], axis=0
        ).astype(jnp.bfloat16)
        found = jnp.dot(side[...], stack, preferred_element_type=jnp.float32)
        column = jnp.where(lane < 64, found[:channels], found[channels:])

        def window(row):
            return jnp.concatenate([hidden[row], hidden[row + 2], hidden[row + 4]], axis=0)

        if not whole_rows:
            out[0, edge : pixel_rows - edge] = inner_ref[0, edge : pixel_rows - edge]
        for first, second in zip(wanted[::2], wanted[1::2]):
            both = jnp.dot(
                taps[...],
                jnp.concatenate([window(first), window(second)], axis=1),
                preferred_element_type=jnp.float32,
            )
            ready = []
            for half, row in enumerate((first, second)):
                parts = both[:, half * pixel_cols : (half + 1) * pixel_cols]
                at = 3 * (row + 2)
                values = (
                    parts[channels : 2 * channels]
                    + jnp.where(
                        lane < 2,
                        pltpu.roll(column, 128 - at, 1),
                        pltpu.roll(parts[:channels], 2, 1),
                    )
                    + jnp.where(
                        lane >= 126,
                        pltpu.roll(column, (189 - at) % 128, 1),
                        pltpu.roll(parts[2 * channels :], 126, 1),
                    )
                )
                ready.append(jnp.maximum(values + bias_two, 0.0).astype(jnp.bfloat16))
            predicted = jnp.dot(
                matrix_ref[...],
                jnp.concatenate(ready, axis=1),
                preferred_element_type=jnp.float32,
            )
            for half, row in enumerate((first, second)):
                misfit = obs[pl.ds(row, bands, stride=pixel_rows), :] - (
                    predicted[:, half * pixel_cols : (half + 1) * pixel_cols] + offset
                )
                total = jnp.sum(misfit * misfit / variance, axis=0, keepdims=True)
                out[0, row : row + 1] = total * mask_ref[row : row + 1].astype(jnp.float32)

    edge_spec = pl.BlockSpec((1, channels, pixel_cols), lambda i: (i, 0, 0))
    line_spec = pl.BlockSpec((SLOTS, channels, pixel_cols), lambda i: (i, 0, 0))
    packed_spec = pl.BlockSpec(
        (1, channels, pixel_cols), lambda i: (members * SLOTS + lax.div(i, PACKED), 0, 0)
    )
    out_spec = pl.BlockSpec((1, pixel_rows, pixel_cols), lambda i: (i, 0, 0))

    def whole(array):
        return pl.BlockSpec(array.shape, lambda i, n=array.ndim: (0,) * n)

    extra = () if whole_rows else (*rows_in, *rows_in, inner)
    extra_specs = [] if whole_rows else [line_spec] * 2 + [packed_spec] * 2 + [out_spec]
    return pl.pallas_call(
        kernel,
        grid=(members,),
        out_shape=jax.ShapeDtypeStruct((members, pixel_rows, pixel_cols), jnp.float32),
        in_specs=[
            pl.BlockSpec(memory_space=pltpu.SMEM),
            pl.BlockSpec((1, row_count, channels, pixel_cols), lambda i: (i, 0, 0, 0)),
        ]
        + [edge_spec] * 4
        + extra_specs
        + [whole(array) for array in fixed],
        out_specs=out_spec,
        scratch_shapes=[
            pltpu.VMEM((pixel_rows + 4, channels, pixel_cols), jnp.bfloat16),
            pltpu.VMEM((3 * channels, 3 * channels), jnp.bfloat16),
            pltpu.VMEM((2 * channels, 3 * channels), jnp.bfloat16),
        ],
        compiler_params=pltpu.CompilerParams(vmem_limit_bytes=8 << 20),
        name="inner_misfits" if whole_rows else "outer_misfits",
    )(borders, held(partial), *sides, *extra, *[held(x) for x in fixed])


def neighbours(axis):
    count = lax.axis_size(axis)
    onward = [(i, i + 1) for i in range(count - 1)]
    return onward, [(j, i) for i, j in onward]


def departures(
    ancestors,
    place,
    targets,
    seats,
    prior_states,
    measured_brightness,
    measured_indicator,
    sensor_error_spread,
    entry_layer_stencil,
    entry_layer_offset,
    middle_layer_stencil,
    middle_layer_offset,
    brightness_matrix,
    brightness_offset,
):
    channels = entry_layer_stencil.shape[0]
    lat, lon = lax.axis_index("lat"), lax.axis_index("lon")
    borders = jnp.stack(
        [lat, lax.axis_size("lat") - 1 - lat, lon, lax.axis_size("lon") - 1 - lon]
    ).astype(jnp.int32)
    members = prior_states.shape[0]
    weights = held(jnp.transpose(entry_layer_stencil, (2, 3, 1, 0)))
    common = (ancestors, place, held(prior_states), weights, targets, seats)
    first = max(1, 3 * members // 8)
    *ends, picked, table, even, odd = entry_layer(*common, (0, first), None)
    partial, own_east, own_west = entry_layer(*common, (first, members), (even, odd, *ends))
    count = lax.axis_size("lon")
    ring = [(i, (i + 1) % count) for i in range(count)]
    from_west = lax.ppermute(own_east, "lon", ring)
    from_east = lax.ppermute(own_west, "lon", [(j, i) for i, j in ring])
    sides = (own_east, own_west, from_west, from_east)
    north, south = row_ends(borders, partial, *sides)
    onward, back = neighbours("lat")
    from_north = lax.ppermute(south, "lat", onward)
    from_south = lax.ppermute(north, "lat", back)
    bands = brightness_matrix.shape[0]
    vectors = jnp.stack(
        [
            entry_layer_offset,
            middle_layer_offset,
            jnp.pad(brightness_offset, (0, channels - bands)),
            jnp.pad(sensor_error_spread, (0, channels - bands), constant_values=1.0),
        ],
        axis=1,
    )
    fixed = (
        vectors,
        jnp.transpose(middle_layer_stencil, (2, 3, 0, 1)),
        brightness_matrix,
        measured_brightness.reshape(-1, measured_brightness.shape[-1]),
        measured_indicator,
    )
    inner = misfits(borders, partial, sides, None, None, fixed)
    squares = misfits(borders, partial, sides, (from_north, from_south), inner, fixed)
    return squares, picked, table, borders


def chunk_of(heights):
    return next(size for size in (5, 4, 2, 1) if heights % size == 0)


def body(prior_states, *rest):
    ancestor_indices = rest[-1]
    members, heights, rows, cols = prior_states.shape
    groups = lax.axis_size("ens")
    own = lax.axis_index("ens").astype(jnp.int32)
    seats = max(2, (members + groups - 1) // groups)
    ancestors = jnp.transpose(ancestor_indices, (1, 2, 0)).reshape(-1, ancestor_indices.shape[0])
    swap = [(0, 1), (1, 0)]
    paired = groups == 2
    if paired:
        targets = (1 - own)[None]
    else:
        targets = jnp.arange(groups, dtype=jnp.int32)
    place = jnp.concatenate([own[None], targets])
    squares, picked, table, borders = departures(
        ancestors, place, targets.shape[0], seats, prior_states, *rest[:-1]
    )
    if paired:
        received = lax.ppermute(picked, "ens", swap)
    else:
        received = lax.all_to_all(picked, "ens", split_axis=0, concat_axis=0, tiled=True)
    band_lat = taper_band(squares.shape[1], RADIUS)
    padded = extended(squares, (("lat", 1),), RADIUS)
    smooth = jnp.einsum("ij,pjk->pik", band_lat, padded, precision=lax.Precision.HIGHEST)
    pixel_cols = squares.shape[2]
    band_lon = np.zeros((3 * pixel_cols, pixel_cols), np.float32)
    near = slice(pixel_cols - RADIUS, 2 * pixel_cols + RADIUS)
    band_lon[near] = taper_band(pixel_cols, RADIUS).T
    count = lax.axis_size("lon")
    ring = [(i, (i + 1) % count) for i in range(count)]
    from_west = lax.ppermute(smooth, "lon", ring)
    from_east = lax.ppermute(smooth, "lon", [(j, i) for i, j in ring])
    size = chunk_of(heights)
    pieces = PIECES if heights // size % PIECES == 0 else 1
    levels = heights // pieces
    field = prior_states
    scaled, own_norm, own_mean, *sent = group_mean(
        borders, smooth, from_west, from_east, band_lon, field, pieces, size
    )
    if paired:
        other_norm = lax.ppermute(own_norm, "ens", swap)
        others = [lax.ppermute(piece, "ens", swap) for piece in sent]
    else:
        peak = lax.pmax(own_norm[0], "ens")
        part = own_norm[1] * jnp.exp(own_norm[0] - peak)
        total, added = lax.psum((part, expand_patches(part)[None] * own_mean), "ens")
        own_mean = added / expand_patches(total)[None]
        other_norm = jnp.stack([peak, total])
        others = sent
    weights, parts = merge(scaled, own_norm, other_norm, not paired)
    analysis = None
    for k, other_mean in enumerate(others):
        analysis = combine(
            table, parts, own_mean, other_mean, field, received, analysis, k * levels, size
        )
    return analysis, weights


def solution(mesh):
    return jax.shard_map(
        body,
        mesh=mesh,
        in_specs=(
            P("ens", None, "lat", "lon"),
            P(None, "lat", "lon"),
            P("lat", "lon"),
            P(),
            P(),
            P(),
            P(),
            P(),
            P(),
            P(),
            P(None, "lat", "lon"),
        ),
        out_specs=(P("ens", None, "lat", "lon"), P("ens", "lat", "lon")),
        check_vma=False,
    )
```
